256 devices in a mesh: clus: 32 (over x, z), sub: 8 (over y, core).
Axes of the slice: x: 4, y: 4, z: 8, core: 2. Of those that a mesh axis runs over, the one named last changes fastest.
Arguments:
- forward_rhs: bfloat16 [1024, 32, 256], P('clus', 'sub'), may hold values from -6 to 6
- adjoint_rhs: bfloat16 [1024, 32, 256], P('clus', 'sub'), may hold values from -6 to 6
- far_clusters: int32 [2, 32768], P(None, ('clus', 'sub')), may hold values from 0 to 1023, as said below
- far_ranks: int32 [32768], P(('clus', 'sub')), may hold values from 0 to 32, as said below
- far_left: bfloat16 [32768, 2, 32, 128], P(('clus', 'sub')), may hold values from -0.25 to 0.25
- far_right: bfloat16 [32768, 2, 32, 128], P(('clus', 'sub')), may hold values from -0.5 to 0.5
- near_clusters: int32 [2, 8192], P(None, ('clus', 'sub')), may hold values from 0 to 1023, as said below
- near_blocks: bfloat16 [8192, 2, 128, 128], P(('clus', 'sub')), may hold values from -0.125 to 0.125
- panel_params: int32 [4, 131072], P(None, 'clus'), may hold values from 0 to 32767, as said below
- panel_weights: float32 [4, 131072], P(None, 'clus'), may hold values from -6 to 6
- panel_counts: int32 [131072], P('clus'), may hold values from 1 to 4
Outputs:
- forward_field: float32 [1024, 32, 256], P('clus', 'sub')
- adjoint_field: float32 [1024, 32, 256], P('clus', 'sub')
- param_gradient: float32 [32768], P(('clus', 'sub'))
The draws below stay inside these ranges and needn't reach their ends.
Inputs may be any that keep to these rules, and one draw needn't show every extreme that they name: `far_clusters`: block slot b belongs to device b // 128; its row cluster lies in row group g = (b // 128) // 8, among clusters 32 * g to 32 * g + 31; its column cluster is the row cluster plus d modulo 1024 with 2 <= |d| <= 32. `far_ranks`: 0 marks an empty slot; on each device the live slots come first. `near_clusters`: block slot b belongs to device b // 32; its row cluster lies in row group (b // 32) // 8; its column cluster is the row cluster plus d modulo 1024 with |d| <= 1. panel_params[0,p] equals p // 4 plus an offset of -3 to 3, modulo 32768; the other slots may name any shape parameter.
All inputs are finite; a program needn't handle non-finite values.
Results may differ from the reference program's by a relative error of at most 0.0036.
Values may be sent and summed in bfloat16 or wider, within the bound.
A program may use at most 128 MiB of HBM per device.

```python
import jax
import jax.numpy as jnp
from jax import lax

CS = 128
RANK = 32
NRHS = 32
PSLOT = 4
CG = 32
FAR_DEV = 128
NEAR_DEV = 32
MEMBERS = 8
NC = 1024
NP = 131072
NPAR = 32768
PPP = 4
FAR_ALL = 32768
NEAR_ALL = 8192


def draw_far_clusters(key, part):
    key_rows, key_magnitude, key_signs = jax.random.split(jax.random.fold_in(key, 11), 3)
    slot_total = FAR_ALL
    flat_index = jnp.arange(slot_total, dtype=jnp.int32)
    group_ids = flat_index // FAR_DEV // MEMBERS
    within_group = jax.random.randint(key_rows, (slot_total,), 0, CG, dtype=jnp.int32)
    within_group = within_group.at[0].set(0).at[slot_total - 1].set(CG - 1)
    row_ids = group_ids * CG + within_group
    offsets = jax.random.randint(key_magnitude, (slot_total,), 2, CG + 1, dtype=jnp.int32)
    signs = jax.random.randint(key_signs, (slot_total,), 0, 2, dtype=jnp.int32) * 2 - 1
    col_ids = (row_ids + offsets * signs) % NC
    return jnp.stack([row_ids, col_ids]).astype(jnp.int32)


def draw_far_ranks(key, part):
    key_live, key_ranks = jax.random.split(jax.random.fold_in(key, 23), 2)
    device_total = FAR_ALL // FAR_DEV
    flat_index = jnp.arange(FAR_ALL, dtype=jnp.int32)
    device_ids = flat_index // FAR_DEV
    slot_ids = flat_index % FAR_DEV
    live_counts = jax.random.randint(key_live, (device_total,), FAR_DEV // 2, FAR_DEV + 1, dtype=jnp.int32)
    live_counts = live_counts.at[0].set(FAR_DEV).at[device_total - 1].set(FAR_DEV // 2)
    rank_draw = jax.random.randint(key_ranks, (FAR_ALL,), 1, RANK + 1, dtype=jnp.int32)
    rank_draw = rank_draw.at[0].set(RANK)
    return jnp.where(slot_ids < live_counts[device_ids], rank_draw, 0).astype(jnp.int32)


def draw_near_clusters(key, part):
    key_rows, key_offsets = jax.random.split(jax.random.fold_in(key, 37), 2)
    slot_total = NEAR_ALL
    flat_index = jnp.arange(slot_total, dtype=jnp.int32)
    group_ids = flat_index // NEAR_DEV // MEMBERS
    within_group = jax.random.randint(key_rows, (slot_total,), 0, CG, dtype=jnp.int32)
    within_group = within_group.at[0].set(0).at[slot_total - 1].set(CG - 1)
    row_ids = group_ids * CG + within_group
    offsets = jax.random.randint(key_offsets, (slot_total,), -1, 2, dtype=jnp.int32)
    offsets = offsets.at[0].set(0).at[slot_total - 1].set(0)
    col_ids = (row_ids + offsets) % NC
    return jnp.stack([row_ids, col_ids]).astype(jnp.int32)


def draw_panel_params(key, part):
    key_offsets, key_global = jax.random.split(jax.random.fold_in(key, 41), 2)
    home_params = jnp.arange(NP, dtype=jnp.int32) // PPP
    offsets = jax.random.randint(key_offsets, (NP,), -3, 4, dtype=jnp.int32)
    local_slot = (home_params + offsets) % NPAR
    global_slots = jax.random.randint(key_global, (PSLOT - 1, NP), 0, NPAR, dtype=jnp.int32)
    global_slots = global_slots.at[0, 0].set(NPAR - 1).at[0, 1].set(0)
    return jnp.concatenate([local_slot[None, :], global_slots], axis=0).astype(jnp.int32)


def draw_panel_counts(key, part):
    key_counts = jax.random.fold_in(key, 53)
    counts = jax.random.randint(key_counts, (NP,), 1, PSLOT + 1, dtype=jnp.int32)
    return counts.at[0].set(PSLOT).at[1].set(PSLOT).at[2].set(1).astype(jnp.int32)


def level_of(own_key, dims, pieces, smallest, top_value):
    gain = 1.0
    for axis_at, shards_of in pieces:
        draws = jax.random.uniform(jax.random.fold_in(jax.random.fold_in(own_key, 6), axis_at), (shards_of,), jnp.float32, smallest / len(pieces), top_value / len(pieces))
        gain = gain * jnp.repeat(jnp.exp(draws), dims[axis_at] // shards_of).reshape((-1,) + (1,) * (len(dims) - 1 - axis_at))
    return gain


def gaussian(stream_key, dims, spread, most, shards=(), held_as=jnp.bfloat16):
    entries = jax.random.normal(stream_key, dims, jnp.float32) * spread
    if len(shards) > 0:
        entries = level_of(stream_key, dims, shards, -0.22, 0.18) * entries
    return jnp.clip(entries, min=-most, max=most).astype(held_as)


def setup_inputs(seed: int = 0) -> dict:
    keys = jax.random.split(jax.random.key(seed), 12)
    forward_rhs = gaussian(keys[0], (NC, NRHS, 2 * CS), 1.0, 6.0, ((0, 32), (1, 8)))
    adjoint_rhs = gaussian(keys[1], (NC, NRHS, 2 * CS), 1.0, 6.0, ((0, 32), (1, 8)))
    far_clusters = draw_far_clusters(jax.random.fold_in(keys[11], 71), 0)
    far_ranks = draw_far_ranks(jax.random.fold_in(keys[11], 71), 0)
    far_left = gaussian(keys[4], (FAR_ALL, 2, RANK, CS), (16 * RANK) ** -0.5, 0.25, ((0, 256),))
    far_right = gaussian(keys[5], (FAR_ALL, 2, RANK, CS), CS ** -0.5, 0.5, ((0, 256),))
    near_clusters = draw_near_clusters(jax.random.fold_in(keys[11], 71), 0)
    near_blocks = gaussian(keys[7], (NEAR_ALL, 2, CS, CS), (16 * CS) ** -0.5, 0.125, ((0, 256),))
    panel_params = draw_panel_params(jax.random.fold_in(keys[11], 71), 0)
    panel_weights = gaussian(keys[9], (PSLOT, NP), 1.0, 6.0, ((1, 32),), jnp.float32)
    panel_counts = draw_panel_counts(jax.random.fold_in(keys[11], 71), 0)
    return {"forward_rhs": forward_rhs, "adjoint_rhs": adjoint_rhs, "far_clusters": far_clusters, "far_ranks": far_ranks, "far_left": far_left, "far_right": far_right, "near_clusters": near_clusters, "near_blocks": near_blocks, "panel_params": panel_params, "panel_weights": panel_weights, "panel_counts": panel_counts}


def complex_mix(lhs_data, rhs_factor, einsum_form):
    width = lhs_data.shape[-1] // 2
    real_lhs = lhs_data[..., :width].astype(jnp.float32)
    imag_lhs = lhs_data[..., width:].astype(jnp.float32)
    real_rhs = rhs_factor[:, 0].astype(jnp.float32)
    imag_rhs = rhs_factor[:, 1].astype(jnp.float32)
    real_out = jnp.einsum(einsum_form, real_lhs, real_rhs) - jnp.einsum(einsum_form, imag_lhs, imag_rhs)
    imag_out = jnp.einsum(einsum_form, real_lhs, imag_rhs) + jnp.einsum(einsum_form, imag_lhs, real_rhs)
    return jnp.concatenate([real_out, imag_out], axis=-1)


def rank_columns(rank_list, width):
    column_ids = lax.broadcasted_iota(jnp.int32, (rank_list.shape[0], width), 1)
    kept = (column_ids < rank_list[:, None]).astype(jnp.float32)
    return jnp.concatenate([kept, kept], axis=1)[:, None, :]


def reference(forward_rhs, adjoint_rhs, far_clusters, far_ranks, far_left, far_right, near_clusters, near_blocks, panel_params, panel_weights, panel_counts):
    cluster_total = forward_rhs.shape[0]
    far_groups = far_ranks.shape[0] // FAR_DEV
    near_groups = near_blocks.shape[0] // NEAR_DEV
    far_pairs = far_clusters.reshape(2, far_groups, FAR_DEV).transpose(1, 0, 2)
    near_pairs = near_clusters.reshape(2, near_groups, NEAR_DEV).transpose(1, 0, 2)

    def far_step(state_pair, batch):
        fwd_acc, adj_acc = state_pair
        pair_ids, rank_list, left_factor, right_factor = batch
        row_ids = pair_ids[0]
        col_ids = pair_ids[1]
        kept = rank_columns(rank_list, left_factor.shape[2])
        coeff = (complex_mix(forward_rhs[col_ids], right_factor, "bkq,bjq->bkj") * kept).astype(jnp.bfloat16)
        coeff = lax.optimization_barrier(coeff)
        fwd_acc = fwd_acc + jax.ops.segment_sum(complex_mix(coeff, left_factor, "bkj,bjp->bkp"), row_ids, num_segments=cluster_total)
        back_coeff = (complex_mix(adjoint_rhs[row_ids], left_factor, "bkp,bjp->bkj") * kept).astype(jnp.bfloat16)
        back_coeff = lax.optimization_barrier(back_coeff)
        adj_acc = adj_acc + jax.ops.segment_sum(complex_mix(back_coeff, right_factor, "bkj,bjq->bkq"), col_ids, num_segments=cluster_total)
        return (fwd_acc, adj_acc), None

    def near_step(state_pair, batch):
        fwd_acc, adj_acc = state_pair
        pair_ids, dense_block = batch
        row_ids = pair_ids[0]
        col_ids = pair_ids[1]
        fwd_acc = fwd_acc + jax.ops.segment_sum(complex_mix(forward_rhs[col_ids], dense_block, "bkq,bpq->bkp"), row_ids, num_segments=cluster_total)
        adj_acc = adj_acc + jax.ops.segment_sum(complex_mix(adjoint_rhs[row_ids], dense_block, "bkp,bpq->bkq"), col_ids, num_segments=cluster_total)
        return (fwd_acc, adj_acc), None

    zero_field = jnp.zeros(forward_rhs.shape, jnp.float32)
    far_batches = (far_pairs, far_ranks.reshape(far_groups, FAR_DEV),
                   far_left.reshape((far_groups, FAR_DEV) + far_left.shape[1:]),
                   far_right.reshape((far_groups, FAR_DEV) + far_right.shape[1:]))
    state_pair, _ = lax.scan(far_step, (zero_field, zero_field), far_batches)
    near_batches = (near_pairs, near_blocks.reshape((near_groups, NEAR_DEV) + near_blocks.shape[1:]))
    state_pair, _ = lax.scan(near_step, state_pair, near_batches)
    forward_field, adjoint_field = state_pair
    half_width = forward_field.shape[-1] // 2
    sensitivity = jnp.sum(forward_field[..., :half_width] * adjoint_field[..., :half_width]
                          - forward_field[..., half_width:] * adjoint_field[..., half_width:], axis=1).reshape(-1) / forward_rhs.shape[1]
    slot_ids = lax.broadcasted_iota(jnp.int32, panel_params.shape, 0)
    live_slots = slot_ids < panel_counts[None, :]
    weighted = jnp.where(live_slots, panel_weights * sensitivity[None, :], jnp.zeros(panel_weights.shape, panel_weights.dtype))
    param_gradient = jax.ops.segment_sum(weighted.reshape(-1), panel_params.reshape(-1), num_segments=NPAR)
    return forward_field, adjoint_field, param_gradient
```

```python
import jax
import jax.numpy as jnp
from jax import lax
from jax.experimental import pallas as pl
from jax.experimental.pallas import tpu as pltpu
from jax.sharding import PartitionSpec as P

MESH = pl.DeviceIdType.MESH
F32 = jnp.float32
BF16 = jnp.bfloat16

GROUPS = 32
MEMBERS = 8
RING = 4
CG = 32
COLS = 4
CS = 128
RANK = 32
FAR = 128
NEAR = 32
STEPS = 8
WIDE = 4 * CG


def place():
    c = lax.axis_index("clus")
    s = lax.axis_index("sub")
    y = s // 2
    p = s % 2
    up, down, far = (y + 1) % RING, (y + 3) % RING, (y + 2) % RING
    return c, s, y, p, up, down, far


def meet(peers):
    barrier = pltpu.get_barrier_semaphore()
    for peer in peers:
        pl.semaphore_signal(barrier, inc=1, device_id=peer, device_id_type=MESH)
    pl.semaphore_wait(barrier, len(peers))


def gather_kernel(x_ref, w_ref, xo, wo, send, recv, local):
    c, s, y, p, up, down, far = place()
    to_up, to_down = {"sub": 2 * up + p}, {"sub": 2 * down + p}
    to_mate = {"sub": 2 * y + 1 - p}
    to_next, to_prev = {"clus": (c + 1) % GROUPS}, {"clus": (c + GROUPS - 1) % GROUPS}
    meet([to_up, to_down, to_mate, to_next, to_prev])

    def copy(src, dst, k, peer):
        return pltpu.make_async_remote_copy(
            src_ref=src, dst_ref=dst, send_sem=send.at[k], recv_sem=recv.at[k], device_id=peer, device_id_type=MESH
        )

    own = pl.ds(CG, CG)
    subs = [2 * t + p for t in (y, down, up, far)]
    mates = [2 * t + 1 - p for t in (y, down, up, far)]

    started = []

    def go(src, dst, k, peer):
        d = copy(src, dst, k, peer)
        d.start()
        started.append(d)

    def arrived(ref, k):
        copy(ref, ref, k, to_mate).wait_recv()

    keep_x = pltpu.make_async_copy(x_ref, xo.at[own, :, s], local.at[0])
    keep_w = pltpu.make_async_copy(w_ref, wo.at[:, :, s], local.at[1])
    go(w_ref, wo.at[:, :, s], 0, to_up)
    go(x_ref, xo.at[own, :, s], 4, to_down)
    go(w_ref, wo.at[:, :, s], 1, to_down)
    go(x_ref, xo.at[own, :, s], 3, to_up)
    go(x_ref, xo.at[pl.ds(0, CG), :, s], 6, to_next)
    go(x_ref, xo.at[pl.ds(2 * CG, CG), :, s], 10, to_prev)
    go(w_ref, wo.at[:, :, s], 14, to_mate)
    go(x_ref, xo.at[own, :, s], 18, to_mate)
    keep_x.start()
    keep_w.start()

    def got_w(i):
        ref = wo.at[:, :, subs[i]]
        arrived(ref, i - 1)
        if i == 2:
            go(ref, ref, 2, to_down)
        go(ref, ref, 14 + i, to_mate)

    def got_x(i):
        ref = xo.at[own, :, subs[i]]
        arrived(ref, 2 + i)
        if i == 1:
            go(ref, ref, 5, to_up)
        go(ref, xo.at[pl.ds(0, CG), :, subs[i]], 6 + i, to_next)
        go(ref, xo.at[pl.ds(2 * CG, CG), :, subs[i]], 10 + i, to_prev)
        go(ref, ref, 18 + i, to_mate)

    def got_side(i):
        left = xo.at[pl.ds(0, CG), :, subs[i]]
        arrived(left, 6 + i)
        go(left, left, 22 + i, to_mate)
        right = xo.at[pl.ds(2 * CG, CG), :, subs[i]]
        arrived(right, 10 + i)
        go(right, right, 26 + i, to_mate)

    got_x(1)
    got_w(2)
    got_x(2)
    got_w(1)
    got_side(0)
    got_x(3)
    got_w(3)
    got_side(1)
    got_side(2)
    got_side(3)
    for i in range(4):
        arrived(wo.at[:, :, mates[i]], 14 + i)
        arrived(xo.at[own, :, mates[i]], 18 + i)
        arrived(xo.at[pl.ds(0, CG), :, mates[i]], 22 + i)
        arrived(xo.at[pl.ds(2 * CG, CG), :, mates[i]], 26 + i)
    for d in started:
        d.wait_send()
    keep_x.wait()
    keep_w.wait()


def real_form(ref, b, sign):
    re, im = ref[b, 0], ref[b, 1]
    if sign > 0:
        top, low = [re, im], [-im, re]
    else:
        top, low = [re, -im], [im, re]
    return jnp.concatenate([jnp.concatenate(top, axis=1), jnp.concatenate(low, axis=1)], axis=0)


NT = (((1,), (1,)), ((), ()))
NN = (((1,), (0,)), ((), ()))


def mm(a, b, dims):
    return lax.dot_general(a, b, dims, preferred_element_type=F32)


def block_kernel(far_ids, ranks, near_ids, x_ref, w_ref, u_ref, v_ref, n_ref, out, acc):
    step = pl.program_id(0)
    first = lax.axis_index("clus") * CG
    total = GROUPS * CG

    @pl.when(step == 0)
    def _():
        acc[...] = jnp.zeros_like(acc)

    def row_of(ids, b):
        return jnp.clip(ids[0, b] - first, 0, CG - 1)

    def col_of(ids, b):
        return jnp.clip((ids[1, b] - first + CG + total) % total, 0, 3 * CG - 1)

    def slot_of(col):
        return jnp.where(col < CG, col, jnp.where(col < 2 * CG, col + CG, col - CG))

    def rows(ref, r, conj):
        re, im = ref[r, 0], ref[r, 1]
        return jnp.concatenate([re, -im if conj else im], axis=1)

    lane = lax.broadcasted_iota(jnp.int32, (1, 256), 1)
    per = FAR // STEPS
    for g in range(per // 4):
        local = [4 * g + i for i in range(4)]
        slots = [step * per + b for b in local]
        r = [row_of(far_ids, b) for b in slots]
        col = [col_of(far_ids, b) for b in slots]
        keep = [((lane // 64 == i) & (lane % RANK < ranks[slots[i]])).astype(F32) for i in range(4)]
        vm = jnp.concatenate([real_form(v_ref, b, -1) for b in local], axis=0)
        um = jnp.concatenate([real_form(u_ref, b, 1) for b in local], axis=0)

        def masked(m):
            parts = [(m[32 * i : 32 * i + 32] * keep[i]).astype(BF16) for i in range(4)]
            return jnp.concatenate(parts, axis=0)

        x4 = jnp.concatenate([rows(x_ref, k, False) for k in col], axis=0)
        w4 = jnp.concatenate([rows(w_ref, k, True) for k in r], axis=0)
        fwd = mm(masked(mm(x4, vm, NT)), um, NN)
        adj = mm(masked(mm(w4, um, NT)), vm, NN)
        for i in range(4):
            acc[3 * CG + r[i]] += fwd[32 * i : 32 * i + 32]
            acc[slot_of(col[i])] += adj[32 * i : 32 * i + 32]
    per = NEAR // STEPS
    for b in range(per):
        slot = step * per + b
        r, col = row_of(near_ids, slot), col_of(near_ids, slot)
        nm = real_form(n_ref, b, -1)
        acc[3 * CG + r] += mm(rows(x_ref, col, False), nm, NT)
        acc[slot_of(col)] += mm(rows(w_ref, r, True), nm, NN)

    @pl.when(step == STEPS - 1)
    def _():
        def one(k, carry):
            a = acc[k]
            out[k, 0] = a[:, :CS].astype(BF16)
            out[k, 1] = a[:, CS:].astype(BF16)
            return carry

        lax.fori_loop(0, WIDE, one, 0)


HALF = 2 * CG


def scatter_kernel(part, fwd, adj, sens, mate_in, mine, pass_in, done_in, side_out, side_in, send, recv):
    c, s, y, p, up, down, far = place()
    to_up, to_down = {"sub": 2 * up + p}, {"sub": 2 * down + p}
    to_mate = {"sub": 2 * y + 1 - p}
    to_next, to_prev = {"clus": (c + 1) % GROUPS}, {"clus": (c + GROUPS - 1) % GROUPS}
    meet([to_up, to_down, to_mate, to_next, to_prev])
    started = []

    def copy(src, dst, k, peer):
        return pltpu.make_async_remote_copy(
            src_ref=src, dst_ref=dst, send_sem=send.at[k], recv_sem=recv.at[k], device_id=peer, device_id_type=MESH
        )

    def go(src, dst, k, peer):
        d = copy(src, dst, k, peer)
        d.start()
        started.append(d)

    def arrived(ref, k):
        copy(ref, ref, k, to_mate).wait_recv()

    tos = [far, up, down, y]
    for ph in range(2):
        for j in range(4):
            go(part.at[pl.ds(ph * HALF, HALF), :, 2 * tos[j] + 1 - p], mate_in.at[ph, j], 4 * ph + j, to_mate)

    chunk = 8

    def pair_sum(ph, j, lo, hi, extra=None):
        who = 2 * tos[j] + p

        def one(i, carry):
            at = pl.ds(lo + i * chunk, chunk)
            a = part[pl.ds(ph * HALF + lo + i * chunk, chunk), :, who].astype(F32) + mate_in[ph, j, at].astype(F32)
            if extra is not None:
                a = a + extra[pl.ds(i * chunk, chunk)].astype(F32)
            mine[ph, j, at] = a.astype(BF16)
            return carry

        lax.fori_loop(0, (hi - lo) // chunk, one, 0)

    A, B = pl.ds(0, CG), pl.ds(CG, CG)
    for ph in range(2):
        base = 8 + 6 * ph
        arrived(mate_in.at[ph, 0], 4 * ph)
        pair_sum(ph, 0, 0, CG)
        go(mine.at[ph, 0, A], pass_in.at[ph, 0], base, to_up)
        pair_sum(ph, 0, CG, HALF)
        go(mine.at[ph, 0, B], pass_in.at[ph, 1], base + 1, to_down)
        arrived(mate_in.at[ph, 1], 4 * ph + 1)
        pair_sum(ph, 1, CG, HALF)
        go(mine.at[ph, 1, B], done_in.at[ph, 0, B], base + 2, to_up)
        arrived(mate_in.at[ph, 2], 4 * ph + 2)
        pair_sum(ph, 2, 0, CG)
        go(mine.at[ph, 2, A], done_in.at[ph, 1, A], base + 3, to_down)
        arrived(pass_in.at[ph, 0], base)
        pair_sum(ph, 1, 0, CG, pass_in.at[ph, 0])
        go(mine.at[ph, 1, A], done_in.at[ph, 0, A], base + 4, to_up)
        arrived(pass_in.at[ph, 1], base + 1)
        pair_sum(ph, 2, CG, HALF, pass_in.at[ph, 1])
        go(mine.at[ph, 2, B], done_in.at[ph, 1, B], base + 5, to_down)

    def finish(ph):
        base = 8 + 6 * ph
        arrived(mate_in.at[ph, 3], 4 * ph + 3)
        arrived(done_in.at[ph, 0, B], base + 2)
        arrived(done_in.at[ph, 1, A], base + 3)
        arrived(done_in.at[ph, 0, A], base + 4)
        arrived(done_in.at[ph, 1, B], base + 5)

    def whole(ph, at, n):
        a = part[pl.ds(ph * HALF + at, n), :, s].astype(F32) + mate_in[ph, 3, pl.ds(at, n)].astype(F32)
        return a + done_in[ph, 0, pl.ds(at, n)].astype(F32) + done_in[ph, 1, pl.ds(at, n)].astype(F32)

    finish(0)

    def edge(i, carry):
        at = i * chunk
        side_out[pl.ds(at, chunk)] = whole(0, at, chunk)
        return carry

    lax.fori_loop(0, CG // chunk, edge, 0)
    go(side_out.at[A], side_in.at[0], 20, to_prev)
    lax.fori_loop(CG // chunk, HALF // chunk, edge, 0)
    go(side_out.at[B], side_in.at[1], 21, to_next)
    finish(1)
    arrived(side_in.at[0], 20)
    arrived(side_in.at[1], 21)

    def last(i, carry):
        at = i * chunk
        here = pl.ds(at, chunk)
        a = whole(1, at, chunk) + side_in[0, here] + side_in[1, here]
        f = whole(1, CG + at, chunk)
        fwd[here] = f
        adj[here, 0] = a[:, 0]
        adj[here, 1] = -a[:, 1]
        prod = f * a
        sens[here] = jnp.sum(prod[:, 0] + prod[:, 1], axis=1) * (1.0 / (MEMBERS * COLS))
        return carry

    lax.fori_loop(0, CG // chunk, last, 0)
    for d in started:
        d.wait_send()


def param_kernel(sens, params, weights, counts, out, grid, got, row, ring, send, recv, send2, recv2):
    c, s, y, p, up, down, far = place()
    barrier = pltpu.get_barrier_semaphore()
    for off in range(1, MEMBERS):
        pl.semaphore_signal(barrier, inc=1, device_id={"sub": (s + off) % MEMBERS}, device_id_type=MESH)

    def tell(off, carry):
        pl.semaphore_signal(barrier, inc=1, device_id={"clus": (c + off) % GROUPS}, device_id_type=MESH)
        return carry

    lax.fori_loop(1, GROUPS, tell, 0)

    devices = GROUPS * MEMBERS
    high = lax.broadcasted_iota(jnp.int32, (devices, CS), 0)
    low = lax.broadcasted_iota(jnp.int32, (CS, CS), 0)
    one, zero = jnp.ones((), F32), jnp.zeros((), F32)

    def cluster(k, total):
        at = pl.multiple_of(k * CS, CS)
        value = sens[pl.ds(k, 1), :]
        count = counts[pl.ds(k, 1), :]
        left, right = [], []
        for m in range(4):
            q = params[pl.ds(m, 1), pl.ds(at, CS)]
            wt = weights[pl.ds(m, 1), pl.ds(at, CS)]
            val = jnp.where(count > m, wt * value, zero)
            top = val.astype(BF16).astype(F32)
            rest = val - top
            owner = q // CS
            owner = (owner % MEMBERS) * GROUPS + owner // MEMBERS
            left.append(jnp.where(high == owner, one, zero).astype(BF16))
            hit = low == q % CS
            right.append(
                jnp.concatenate(
                    [jnp.where(hit, top, zero).astype(BF16), jnp.where(hit, rest, zero).astype(BF16)], axis=0
                )
            )
        g = mm(jnp.concatenate(left, axis=1), jnp.concatenate(right, axis=1), NT)
        return total + (g[:, :CS] + g[:, CS:])

    grid[...] = lax.fori_loop(0, CG, cluster, jnp.zeros((devices, CS), F32))
    pl.semaphore_wait(barrier, MEMBERS - 1 + GROUPS - 1)

    def part_of(member):
        return grid.at[pl.ds(pl.multiple_of(member * GROUPS, GROUPS), GROUPS)]

    sent = []
    for off in range(1, MEMBERS):
        to = (s + off) % MEMBERS
        d = pltpu.make_async_remote_copy(
            src_ref=part_of(to), dst_ref=got.at[off - 1], send_sem=send.at[off - 1], recv_sem=recv.at[off - 1],
            device_id={"sub": to}, device_id_type=MESH,
        )
        d.start()
        sent.append(d)
    total = grid[pl.ds(pl.multiple_of(s * GROUPS, GROUPS), GROUPS), :]
    for d in sent:
        d.wait_recv()
    for off in range(MEMBERS - 1):
        total = total + got[off]
    for k in range(GROUPS):
        row[k] = total[k : k + 1]

    def copy(off):
        return pltpu.make_async_remote_copy(
            src_ref=row.at[(c + off) % GROUPS], dst_ref=ring.at[off - 1], send_sem=send2.at[off - 1],
            recv_sem=recv2.at[off - 1], device_id={"clus": (c + off) % GROUPS}, device_id_type=MESH,
        )

    def start(off, carry):
        copy(off).start()
        return carry

    def wait(off, carry):
        copy(off).wait()
        return carry

    lax.fori_loop(1, GROUPS, start, 0)
    for d in sent:
        d.wait_send()
    lax.fori_loop(1, GROUPS, wait, 0)
    final = row[c]
    for k in range(GROUPS - 1):
        final = final + ring[k]
    out[...] = final


ANY = pl.BlockSpec(memory_space=pl.ANY)
VMEM = pl.BlockSpec(memory_space=pltpu.VMEM)


def split_form(x):
    n = x.shape[0]
    return x.reshape(n, COLS, 2, CS).transpose(0, 2, 1, 3)


def joined(x):
    n = x.shape[0]
    return x.transpose(0, 2, 1, 3).reshape(n, COLS, 2 * CS)


def shards(x, w, far_ids, ranks, far_left, far_right, near_ids, near, params, weights, counts):
    wide_x, wide_w = pl.pallas_call(
        gather_kernel,
        out_shape=(
            jax.ShapeDtypeStruct((3 * CG, 2, MEMBERS, COLS, CS), BF16),
            jax.ShapeDtypeStruct((CG, 2, MEMBERS, COLS, CS), BF16),
        ),
        in_specs=[VMEM, VMEM],
        out_specs=(ANY, ANY),
        scratch_shapes=[
            pltpu.SemaphoreType.DMA((30,)),
            pltpu.SemaphoreType.DMA((30,)),
            pltpu.SemaphoreType.DMA((2,)),
        ],
        compiler_params=pltpu.CompilerParams(collective_id=0, has_side_effects=True),
        name="gather",
    )(split_form(x), split_form(w))
    wide_x = wide_x.reshape(3 * CG, 2, MEMBERS * COLS, CS)
    wide_w = wide_w.reshape(CG, 2, MEMBERS * COLS, CS)

    per, pern = FAR // STEPS, NEAR // STEPS
    part = pl.pallas_call(
        block_kernel,
        out_shape=jax.ShapeDtypeStruct((WIDE, 2, MEMBERS * COLS, CS), BF16),
        grid_spec=pltpu.PrefetchScalarGridSpec(
            num_scalar_prefetch=3,
            grid=(STEPS,),
            in_specs=[
                VMEM,
                VMEM,
                pl.BlockSpec((per, 2, RANK, CS), lambda i, *_: (i, 0, 0, 0)),
                pl.BlockSpec((per, 2, RANK, CS), lambda i, *_: (i, 0, 0, 0)),
                pl.BlockSpec((pern, 2, CS, CS), lambda i, *_: (i, 0, 0, 0)),
            ],
            out_specs=VMEM,
            scratch_shapes=[pltpu.VMEM((WIDE, MEMBERS * COLS, 2 * CS), F32)],
        ),
        compiler_params=pltpu.CompilerParams(vmem_limit_bytes=40 << 20),
        name="blocks",
    )(far_ids, ranks, near_ids, wide_x, wide_w, far_left, far_right, near)
    part = part.reshape(WIDE, 2, MEMBERS, COLS, CS)

    fwd, adj, sens = pl.pallas_call(
        scatter_kernel,
        out_shape=(
            jax.ShapeDtypeStruct((CG, 2, COLS, CS), F32),
            jax.ShapeDtypeStruct((CG, 2, COLS, CS), F32),
            jax.ShapeDtypeStruct((CG, CS), F32),
        ),
        in_specs=[VMEM],
        out_specs=(VMEM, VMEM, VMEM),
        scratch_shapes=[
            pltpu.VMEM((2, 4, HALF, 2, COLS, CS), BF16),
            pltpu.VMEM((2, 3, HALF, 2, COLS, CS), BF16),
            pltpu.VMEM((2, 2, CG, 2, COLS, CS), BF16),
            pltpu.VMEM((2, 2, HALF, 2, COLS, CS), BF16),
            pltpu.VMEM((HALF, 2, COLS, CS), F32),
            pltpu.VMEM((2, CG, 2, COLS, CS), F32),
            pltpu.SemaphoreType.DMA((22,)),
            pltpu.SemaphoreType.DMA((22,)),
        ],
        compiler_params=pltpu.CompilerParams(collective_id=1, has_side_effects=True, vmem_limit_bytes=40 << 20),
        name="scatter",
    )(part)

    grad = pl.pallas_call(
        param_kernel,
        out_shape=jax.ShapeDtypeStruct((1, CS), F32),
        in_specs=[VMEM] * 4,
        out_specs=VMEM,
        scratch_shapes=[
            pltpu.VMEM((GROUPS * MEMBERS, CS), F32),
            pltpu.VMEM((MEMBERS - 1, GROUPS, CS), F32),
            pltpu.VMEM((GROUPS, 1, CS), F32),
            pltpu.VMEM((GROUPS - 1, 1, CS), F32),
            pltpu.SemaphoreType.DMA((MEMBERS - 1,)),
            pltpu.SemaphoreType.DMA((MEMBERS - 1,)),
            pltpu.SemaphoreType.DMA((GROUPS - 1,)),
            pltpu.SemaphoreType.DMA((GROUPS - 1,)),
        ],
        compiler_params=pltpu.CompilerParams(collective_id=2, has_side_effects=True),
        name="params",
    )(sens, params, weights, counts.reshape(CG, CS))
    return joined(fwd), joined(adj), grad.reshape(CS)


def solution(mesh):
    rhs = P("clus", "sub", None)
    blocks = P(("clus", "sub"), None, None, None)
    both = ("clus", "sub")
    in_specs = (rhs, rhs, P(None, both), P(both), blocks, blocks, P(None, both), blocks)
    in_specs += (P(None, "clus"), P(None, "clus"), P("clus"))
    out_specs = (rhs, rhs, P(both))
    return jax.shard_map(shards, mesh=mesh, in_specs=in_specs, out_specs=out_specs, check_vma=False)
```

```python
import jax
import jax.numpy as jnp
from jax import lax
from jax.experimental import pallas as pl
from jax.experimental.pallas import tpu as pltpu
from jax.sharding import PartitionSpec as P

MESH = pl.DeviceIdType.MESH
F32 = jnp.float32
BF16 = jnp.bfloat16

GROUPS = 32
MEMBERS = 8
RING = 4
CG = 32
COLS = 4
CS = 128
RANK = 32
FAR = 128
NEAR = 32
SEGS = 4
WIDE = 4 * CG


def place():
    c = lax.axis_index("clus")
    s = lax.axis_index("sub")
    y = s // 2
    p = s % 2
    up, down, far = (y + 1) % RING, (y + 3) % RING, (y + 2) % RING
    return c, s, y, p, up, down, far


NT = (((1,), (1,)), ((), ()))
NN = (((1,), (0,)), ((), ()))


def mm(a, b, dims):
    return lax.dot_general(a, b, dims, preferred_element_type=F32)


def real_form(ref, b, sign):
    re, im = ref[b, 0], ref[b, 1]
    if sign > 0:
        top, low = [re, im], [-im, re]
    else:
        top, low = [re, -im], [im, re]
    return jnp.concatenate([jnp.concatenate(top, axis=1), jnp.concatenate(low, axis=1)], axis=0)


def rows(ref, r, conj):
    re, im = ref[r, 0], ref[r, 1]
    return jnp.concatenate([re, -im if conj else im], axis=1)


PHASES = ((0, 2 * CG), (2 * CG, CG), (3 * CG, CG))


def kernel(
    x_ref, w_ref, u_hbm, v_hbm, n_hbm, far_ids, ranks, near_ids, params, weights, counts,
    fwd, adj, grad,
    xo, wo, u_ref, v_ref, n_ref, ids, table, lists, prod, nprod, part, mate_in, mine, pass_in, done_in,
    side_out, side_in, sens, high_hot, low_hot, grid, got, row, ring,
    local, gsend, grecv, send, recv, psend, precv, csend, crecv,
):
    c, s, y, p, up, down, far = place()
    to_up, to_down = {"sub": 2 * up + p}, {"sub": 2 * down + p}
    to_mate = {"sub": 2 * y + 1 - p}
    to_next, to_prev = {"clus": (c + 1) % GROUPS}, {"clus": (c + GROUPS - 1) % GROUPS}
    barrier = pltpu.get_barrier_semaphore()

    def tell_sub(off, carry):
        pl.semaphore_signal(barrier, inc=1, device_id={"sub": (s + off) % MEMBERS}, device_id_type=MESH)
        return carry

    def tell_clus(off, carry):
        pl.semaphore_signal(barrier, inc=1, device_id={"clus": (c + off) % GROUPS}, device_id_type=MESH)
        return carry

    lax.fori_loop(1, MEMBERS, tell_sub, 0)
    lax.fori_loop(1, GROUPS, tell_clus, 0)

    own = pl.ds(CG, CG)
    keep = [
        pltpu.make_async_copy(w_ref, wo.at[:, :, s], local.at[0]),
        pltpu.make_async_copy(x_ref, xo.at[own, :, s], local.at[1]),
        pltpu.make_async_copy(u_hbm, u_ref, local.at[2]),
        pltpu.make_async_copy(v_hbm, v_ref, local.at[3]),
        pltpu.make_async_copy(n_hbm, n_ref, local.at[4]),
    ]
    for d in keep:
        d.start()

    first = c * CG
    total = GROUPS * CG
    big = 127
    ids[...] = jnp.full_like(ids, -1)
    ids[0:2, :] = far_ids[...]
    ids[2:4, 0:NEAR] = near_ids[...]
    sub_i = lax.broadcasted_iota(jnp.int32, (FAR, FAR), 0)
    lane_i = lax.broadcasted_iota(jnp.int32, (FAR, FAR), 1)
    slot_row = lax.broadcasted_iota(jnp.int32, (1, FAR), 1)
    table[...] = jnp.zeros_like(table)

    def order(key, payload, at, end_at):
        k = jnp.broadcast_to(key, (FAR, FAR))
        kt = k.T
        tie = (k == kt) & (lane_i < sub_i)
        ones = jnp.ones_like(k)
        zeros = jnp.zeros_like(k)
        rank = jnp.sum(jnp.where((k < kt) | tie, ones, zeros), axis=1, keepdims=True)
        opens = jnp.sum(jnp.where(tie, ones, zeros), axis=1, keepdims=True) == 0
        pay = jnp.broadcast_to(payload, (FAR, FAR)).T + jnp.where(opens, 1 << 20, 0)
        table[pl.ds(at, 1), :] = jnp.sum(jnp.where(rank == lane_i, pay, zeros), axis=0, keepdims=True)
        upto = jnp.sum(jnp.where(kt <= lane_i, ones, zeros), axis=0, keepdims=True)
        below = jnp.sum(jnp.where(kt < lane_i, ones, zeros), axis=0, keepdims=True)
        table[pl.ds(end_at, 1), :] = jnp.where(upto > below, upto, 0)

    for i, count in ((0, FAR), (1, NEAR)):
        live = slot_row < count
        r = jnp.clip(ids[2 * i : 2 * i + 1, :] - first, 0, CG - 1)
        q = jnp.clip((ids[2 * i + 1 : 2 * i + 2, :] - first + CG + total) % total, 0, 3 * CG - 1)
        payload = slot_row + q * 128 + r * 16384
        order(jnp.where(live, q, big), payload, 2 * i, 5 + 2 * i)
        order(jnp.where(live, r, big), payload, 2 * i + 1, 6 + 2 * i)
    table[4:5, :] = ranks[...]
    to_lists = pltpu.make_async_copy(table, lists, local.at[5])
    to_lists.start()

    pl.semaphore_wait(barrier, MEMBERS - 1 + GROUPS - 1)

    subs = [2 * t + p for t in (y, down, up, far)]
    mates = [2 * t + 1 - p for t in (y, down, up, far)]
    started = []

    def gcopy(src, dst, k, peer):
        return pltpu.make_async_remote_copy(
            src_ref=src, dst_ref=dst, send_sem=gsend.at[k], recv_sem=grecv.at[k], device_id=peer, device_id_type=MESH
        )

    def ggo(src, dst, k, peer):
        d = gcopy(src, dst, k, peer)
        d.start()
        started.append(d)

    def garrived(ref, k):
        gcopy(ref, ref, k, to_mate).wait_recv()

    left_x, right_x = pl.ds(0, CG), pl.ds(2 * CG, CG)
    ggo(w_ref, wo.at[:, :, s], 0, to_up)
    ggo(w_ref, wo.at[:, :, s], 1, to_down)
    ggo(w_ref, wo.at[:, :, s], 14, to_mate)
    ggo(x_ref, xo.at[left_x, :, s], 6, to_next)
    ggo(x_ref, xo.at[right_x, :, s], 10, to_prev)
    ggo(x_ref, xo.at[own, :, s], 3, to_up)
    ggo(x_ref, xo.at[own, :, s], 4, to_down)
    ggo(x_ref, xo.at[own, :, s], 18, to_mate)

    def got_w(i):
        ref = wo.at[:, :, subs[i]]
        garrived(ref, i - 1)
        if i == 2:
            ggo(ref, ref, 2, to_down)
        ggo(ref, ref, 14 + i, to_mate)

    def got_x(i):
        ref = xo.at[own, :, subs[i]]
        garrived(ref, 2 + i)
        if i == 1:
            ggo(ref, ref, 5, to_up)
        ggo(ref, xo.at[left_x, :, subs[i]], 6 + i, to_next)
        ggo(ref, xo.at[right_x, :, subs[i]], 10 + i, to_prev)
        ggo(ref, ref, 18 + i, to_mate)

    def got_side(i):
        left = xo.at[left_x, :, subs[i]]
        garrived(left, 6 + i)
        ggo(left, left, 22 + i, to_mate)
        right = xo.at[right_x, :, subs[i]]
        garrived(right, 10 + i)
        ggo(right, right, 26 + i, to_mate)

    devices = GROUPS * MEMBERS
    high = lax.broadcasted_iota(jnp.int32, (devices, CS), 0)
    low = lax.broadcasted_iota(jnp.int32, (CS, CS), 0)
    one, zero = jnp.ones((), F32), jnp.zeros((), F32)

    def hot(k, carry):
        at = pl.multiple_of(k * CS, CS)
        for m in range(4):
            q = params[pl.ds(m, 1), pl.ds(at, CS)]
            owner = q // CS
            owner = (owner % MEMBERS) * GROUPS + owner // MEMBERS
            high_hot[k, :, m * CS : m * CS + CS] = jnp.where(high == owner, one, zero).astype(BF16)
            low_hot[k, :, m * CS : m * CS + CS] = jnp.where(low == q % CS, one, zero).astype(BF16)
        return carry

    lax.fori_loop(0, CG // 2, hot, 0)
    got_w(2)
    got_w(1)
    got_x(1)
    got_x(2)
    lax.fori_loop(CG // 2, CG, hot, 0)
    got_w(3)
    got_side(0)
    to_lists.wait()
    keep[0].wait()
    keep[2].wait()
    keep[3].wait()
    for i in range(4):
        garrived(wo.at[:, :, mates[i]], 14 + i)

    xr = xo.reshape(3 * CG, 2, MEMBERS * COLS, CS)
    wr = wo.reshape(CG, 2, MEMBERS * COLS, CS)
    parts = part.reshape(WIDE, 2, MEMBERS * COLS, CS)
    lane = lax.broadcasted_iota(jnp.int32, (1, 256), 1)

    def decode(t):
        b = t % 128
        q = (t // 128) % 128
        r = (t // 16384) % 64
        fresh = (t // (1 << 20)) % 2
        return b, jnp.minimum(q, 3 * CG - 1), jnp.minimum(r, CG - 1), (1 - fresh).astype(F32)

    def far_group(g, run, forward):
        got_t = [decode(lists[1 if forward else 0, 4 * g + i]) for i in range(4)]
        keepers = [((lane // 64 == i) & (lane % RANK < lists[4, got_t[i][0]])).astype(F32) for i in range(4)]
        vm = jnp.concatenate([real_form(v_ref, t[0], -1) for t in got_t], axis=0)
        um = jnp.concatenate([real_form(u_ref, t[0], 1) for t in got_t], axis=0)
        if forward:
            src = jnp.concatenate([rows(xr, t[1], False) for t in got_t], axis=0)
            inner, outer = vm, um
        else:
            src = jnp.concatenate([rows(wr, t[2], True) for t in got_t], axis=0)
            inner, outer = um, vm
        m = mm(src, inner, NT)
        m = jnp.concatenate([(m[32 * i : 32 * i + 32] * keepers[i]).astype(BF16) for i in range(4)], axis=0)
        z = mm(m, outer, NN)
        for i in range(4):
            run = z[32 * i : 32 * i + 32] + got_t[i][3] * run
            prod[4 * g + i] = run
        return run

    def near_block(i, run, forward):
        b, q, r, cont = decode(lists[3 if forward else 2, i])
        b = jnp.minimum(b, NEAR - 1)
        nm = real_form(n_ref, b, -1)
        z = mm(rows(xr, q, False), nm, NT) if forward else mm(rows(wr, r, True), nm, NN)
        run = z + cont * run
        nprod[i] = run
        return run

    blank = jnp.zeros((MEMBERS * COLS, 2 * CS), F32)
    FU, NU = 2, 4

    def far_segment(seg, run, forward):
        n = FAR // 4 // SEGS // FU

        def step(i, run):
            for h in range(FU):
                run = far_group((seg * n + i) * FU + h, run, forward)
            return run

        return lax.fori_loop(0, n, step, run)

    def near_all(forward):
        def step(i, run):
            for h in range(NU):
                run = near_block(i * NU + h, run, forward)
            return run

        lax.fori_loop(0, NEAR // NU, step, blank)

    def collect(lo, hi, shift, far_end, near_end):
        def step(i, carry):
            for h in range(4):
                k = lo + i * 4 + h
                e, n = lists[far_end, k + shift], lists[near_end, k + shift]
                a = prod[jnp.maximum(e - 1, 0)] * jnp.minimum(e, 1).astype(F32)
                a = a + nprod[jnp.clip(n - 1, 0, NEAR - 1)] * jnp.minimum(n, 1).astype(F32)
                parts[k, 0] = a[:, :CS]
                parts[k, 1] = a[:, CS:]
            return carry

        lax.fori_loop(0, (hi - lo) // 4, step, 0)

    run = far_segment(0, blank, False)
    got_x(3)
    run = far_segment(1, run, False)
    got_side(1)
    run = far_segment(2, run, False)
    got_side(2)
    run = far_segment(3, run, False)
    got_side(3)
    keep[4].wait()
    near_all(False)

    def copy(src, dst, k, peer):
        return pltpu.make_async_remote_copy(
            src_ref=src, dst_ref=dst, send_sem=send.at[k], recv_sem=recv.at[k], device_id=peer, device_id_type=MESH
        )

    def go(src, dst, k, peer):
        d = copy(src, dst, k, peer)
        d.start()
        started.append(d)

    def arrived(ref, k):
        copy(ref, ref, k, to_mate).wait_recv()

    tos = [far, up, down, y]
    chunk = 8

    def to_the_mate(ph):
        at = pl.ds(*PHASES[ph])
        for j in range(4):
            go(part.at[at, :, 2 * tos[j] + 1 - p], mate_in.at[j, at], 10 * ph + j, to_mate)

    def pair_sum(j, lo, n, extra=None):
        who = 2 * tos[j] + p

        def step(i, carry):
            at = pl.ds(lo + i * chunk, chunk)
            a = part[at, :, who] + mate_in[j, at]
            if extra is not None:
                a = a + pass_in[extra, at].astype(F32)
            mine[j, at] = a.astype(BF16)
            return carry

        lax.fori_loop(0, n // chunk, step, 0)

    def halves(ph):
        lo, n = PHASES[ph]
        n = n // 2
        return lo, lo + n, n, pl.ds(lo, n), pl.ds(lo + n, n), 10 * ph + 4

    def open_phase(ph):
        a, b, n, at_a, at_b, k = halves(ph)
        everything = pl.ds(*PHASES[ph])
        arrived(mate_in.at[0, everything], 10 * ph)
        pair_sum(0, a, n)
        go(mine.at[0, at_a], pass_in.at[0, at_a], k, to_up)
        pair_sum(0, b, n)
        go(mine.at[0, at_b], pass_in.at[1, at_b], k + 1, to_down)
        arrived(mate_in.at[1, everything], 10 * ph + 1)
        pair_sum(1, b, n)
        go(mine.at[1, at_b], done_in.at[0, at_b], k + 2, to_up)
        arrived(mate_in.at[2, everything], 10 * ph + 2)
        pair_sum(2, a, n)
        go(mine.at[2, at_a], done_in.at[1, at_a], k + 3, to_down)

    def pass_phase(ph):
        a, b, n, at_a, at_b, k = halves(ph)
        arrived(pass_in.at[0, at_a], k)
        pair_sum(1, a, n, 0)
        go(mine.at[1, at_a], done_in.at[0, at_a], k + 4, to_up)
        arrived(pass_in.at[1, at_b], k + 1)
        pair_sum(2, b, n, 1)
        go(mine.at[2, at_b], done_in.at[1, at_b], k + 5, to_down)

    def close_phase(ph):
        a, b, n, at_a, at_b, k = halves(ph)
        arrived(mate_in.at[3, pl.ds(*PHASES[ph])], 10 * ph + 3)
        arrived(done_in.at[0, at_b], k + 2)
        arrived(done_in.at[1, at_a], k + 3)
        arrived(done_in.at[0, at_a], k + 4)
        arrived(done_in.at[1, at_b], k + 5)

    def whole(at):
        a = part[at, :, s] + mate_in[3, at]
        return a + done_in[0, at].astype(F32) + done_in[1, at].astype(F32)

    collect(0, CG, 0, 5, 7)
    collect(CG, 2 * CG, CG, 5, 7)
    to_the_mate(0)
    collect(2 * CG, 3 * CG, -CG, 5, 7)
    to_the_mate(1)
    open_phase(0)
    keep[1].wait()
    for i in range(4):
        garrived(xo.at[own, :, mates[i]], 18 + i)
        garrived(xo.at[left_x, :, mates[i]], 22 + i)
        garrived(xo.at[right_x, :, mates[i]], 26 + i)
    open_phase(1)

    run = far_segment(0, blank, True)
    run = far_segment(1, run, True)
    pass_phase(0)
    run = far_segment(2, run, True)
    pass_phase(1)
    run = far_segment(3, run, True)
    near_all(True)
    collect(3 * CG, 4 * CG, -3 * CG, 6, 8)
    to_the_mate(2)
    close_phase(0)

    def edge(i, carry):
        at = pl.ds(i * chunk, chunk)
        side_out[at] = whole(at)
        return carry

    lax.fori_loop(0, CG // chunk, edge, 0)
    go(side_out.at[pl.ds(0, CG)], side_in.at[0], 30, to_prev)
    lax.fori_loop(CG // chunk, 2 * CG // chunk, edge, 0)
    go(side_out.at[pl.ds(CG, CG)], side_in.at[1], 31, to_next)
    open_phase(2)
    close_phase(1)
    pass_phase(2)
    arrived(side_in.at[0], 30)
    arrived(side_in.at[1], 31)

    def own_adjoint(i, carry):
        at = i * chunk
        here = pl.ds(at, chunk)
        a = whole(pl.ds(2 * CG + at, chunk)) + side_in[0, here] + side_in[1, here]
        adj[here, 0] = a[:, 0]
        adj[here, 1] = -a[:, 1]
        return carry

    lax.fori_loop(0, CG // chunk, own_adjoint, 0)
    close_phase(2)

    def last(i, carry):
        here = pl.ds(i * chunk, chunk)
        f = whole(pl.ds(3 * CG + i * chunk, chunk))
        fwd[here] = f
        prd = f[:, 0] * adj[here, 0] - f[:, 1] * adj[here, 1]
        sens[here] = jnp.sum(prd, axis=1) * (1.0 / (MEMBERS * COLS))
        return carry

    lax.fori_loop(0, CG // chunk, last, 0)

    def cluster(k, carry):
        at = pl.multiple_of(k * CS, CS)
        value = sens[pl.ds(k, 1), :]
        count = counts[pl.ds(k, 1), :]
        tops, rests = [], []
        for m in range(4):
            wt = weights[pl.ds(m, 1), pl.ds(at, CS)]
            val = jnp.where(count > m, wt * value, zero)
            top = val.astype(BF16).astype(F32)
            here = low_hot[k, :, m * CS : m * CS + CS]
            tops.append(here * jnp.broadcast_to(top, (CS, CS)).astype(BF16))
            rests.append(here * jnp.broadcast_to(val - top, (CS, CS)).astype(BF16))
        hits = jnp.concatenate([jnp.concatenate(tops, axis=1), jnp.concatenate(rests, axis=1)], axis=0)
        g = mm(high_hot[k], hits, NT)
        return carry + (g[:, :CS] + g[:, CS:])

    grid[...] = lax.fori_loop(0, CG, cluster, jnp.zeros((devices, CS), F32))

    def part_of(member):
        return grid.at[pl.ds(pl.multiple_of(member * GROUPS, GROUPS), GROUPS)]

    sent = []
    for off in range(1, MEMBERS):
        to = (s + off) % MEMBERS
        d = pltpu.make_async_remote_copy(
            src_ref=part_of(to), dst_ref=got.at[off - 1], send_sem=psend.at[off - 1], recv_sem=precv.at[off - 1],
            device_id={"sub": to}, device_id_type=MESH,
        )
        d.start()
        sent.append(d)
    all_rows = grid[pl.ds(pl.multiple_of(s * GROUPS, GROUPS), GROUPS), :]
    for d in sent:
        d.wait_recv()
    for off in range(MEMBERS - 1):
        all_rows = all_rows + got[off]
    for k in range(GROUPS):
        row[k] = all_rows[k : k + 1]

    def ccopy(off):
        return pltpu.make_async_remote_copy(
            src_ref=row.at[(c + off) % GROUPS], dst_ref=ring.at[off - 1], send_sem=csend.at[off - 1],
            recv_sem=crecv.at[off - 1], device_id={"clus": (c + off) % GROUPS}, device_id_type=MESH,
        )

    def start(off, carry):
        ccopy(off).start()
        return carry

    def wait(off, carry):
        ccopy(off).wait()
        return carry

    lax.fori_loop(1, GROUPS, start, 0)
    for d in sent + started:
        d.wait_send()
    lax.fori_loop(1, GROUPS, wait, 0)
    final = row[c]
    for k in range(GROUPS - 1):
        final = final + ring[k]
    grad[...] = final


ANY = pl.BlockSpec(memory_space=pl.ANY)
VMEM = pl.BlockSpec(memory_space=pltpu.VMEM)


def split_form(x):
    n = x.shape[0]
    return x.reshape(n, COLS, 2, CS).transpose(0, 2, 1, 3)


def joined(x):
    n = x.shape[0]
    return x.transpose(0, 2, 1, 3).reshape(n, COLS, 2 * CS)


def shards(x, w, far_ids, ranks, far_left, far_right, near_ids, near, params, weights, counts):
    def sems(n):
        return pltpu.SemaphoreType.DMA((n,))

    half = (2, COLS, CS)
    fwd, adj, grad = pl.pallas_call(
        kernel,
        out_shape=(
            jax.ShapeDtypeStruct((CG,) + half, F32),
            jax.ShapeDtypeStruct((CG,) + half, F32),
            jax.ShapeDtypeStruct((1, CS), F32),
        ),
        in_specs=[ANY] * 5 + [VMEM] * 6,
        out_specs=(VMEM, VMEM, VMEM),
        scratch_shapes=[
            pltpu.VMEM((3 * CG, 2, MEMBERS, COLS, CS), BF16),
            pltpu.VMEM((CG, 2, MEMBERS, COLS, CS), BF16),
            pltpu.VMEM((FAR, 2, RANK, CS), BF16),
            pltpu.VMEM((FAR, 2, RANK, CS), BF16),
            pltpu.VMEM((NEAR, 2, CS, CS), BF16),
            pltpu.VMEM((8, FAR), jnp.int32),
            pltpu.VMEM((16, FAR), jnp.int32),
            pltpu.SMEM((16, FAR), jnp.int32),
            pltpu.VMEM((FAR, MEMBERS * COLS, 2 * CS), F32),
            pltpu.VMEM((NEAR, MEMBERS * COLS, 2 * CS), F32),
            pltpu.VMEM((WIDE, 2, MEMBERS, COLS, CS), F32),
            pltpu.VMEM((4, WIDE) + half, F32),
            pltpu.VMEM((3, WIDE) + half, BF16),
            pltpu.VMEM((2, WIDE) + half, BF16),
            pltpu.VMEM((2, WIDE) + half, BF16),
            pltpu.VMEM((2 * CG,) + half, F32),
            pltpu.VMEM((2, CG) + half, F32),
            pltpu.VMEM((CG, CS), F32),
            pltpu.VMEM((CG, GROUPS * MEMBERS, 4 * CS), BF16),
            pltpu.VMEM((CG, CS, 4 * CS), BF16),
            pltpu.VMEM((GROUPS * MEMBERS, CS), F32),
            pltpu.VMEM((MEMBERS - 1, GROUPS, CS), F32),
            pltpu.VMEM((GROUPS, 1, CS), F32),
            pltpu.VMEM((GROUPS - 1, 1, CS), F32),
            sems(6),
            sems(30),
            sems(30),
            sems(32),
            sems(32),
            sems(MEMBERS - 1),
            sems(MEMBERS - 1),
            sems(GROUPS - 1),
            sems(GROUPS - 1),
        ],
        compiler_params=pltpu.CompilerParams(collective_id=0, has_side_effects=True, vmem_limit_bytes=60 << 20),
        name="operator",
    )(
        split_form(x), split_form(w), far_left, far_right, near, far_ids, ranks.reshape(1, FAR), near_ids,
        params, weights, counts.reshape(CG, CS),
    )
    return joined(fwd), joined(adj), grad.reshape(CS)


def solution(mesh):
    rhs = P("clus", "sub", None)
    blocks = P(("clus", "sub"), None, None, None)
    both = ("clus", "sub")
    in_specs = (rhs, rhs, P(None, both), P(both), blocks, blocks, P(None, both), blocks)
    in_specs += (P(None, "clus"), P(None, "clus"), P("clus"))
    out_specs = (rhs, rhs, P(both))
    return jax.shard_map(shards, mesh=mesh, in_specs=in_specs, out_specs=out_specs, check_vma=False)
```

```python
import jax
import jax.numpy as jnp
from jax import lax
from jax.experimental import pallas as pl
from jax.experimental.pallas import tpu as pltpu
from jax.sharding import PartitionSpec as P

MESH = pl.DeviceIdType.MESH
F32 = jnp.float32
BF16 = jnp.bfloat16

GROUPS = 32
MEMBERS = 8
RING = 4
CG = 32
COLS = 4
CS = 128
RANK = 32
FAR = 128
NEAR = 32
SEGS = 2
WIDE = 4 * CG


def place():
    c = lax.axis_index("clus")
    s = lax.axis_index("sub")
    y = s // 2
    p = s % 2
    up, down, far = (y + 1) % RING, (y + 3) % RING, (y + 2) % RING
    return c, s, y, p, up, down, far


NT = (((1,), (1,)), ((), ()))
NN = (((1,), (0,)), ((), ()))


def mm(a, b, dims):
    return lax.dot_general(a, b, dims, preferred_element_type=F32)


def real_form(ref, b, sign):
    re, im = ref[b, 0], ref[b, 1]
    if sign > 0:
        top, low = [re, im], [-im, re]
    else:
        top, low = [re, -im], [im, re]
    return jnp.concatenate([jnp.concatenate(top, axis=1), jnp.concatenate(low, axis=1)], axis=0)


def rows(ref, r, conj):
    re, im = ref[r, 0], ref[r, 1]
    return jnp.concatenate([re, -im if conj else im], axis=1)


def cols(member):
    return pl.ds(pl.multiple_of(COLS * member, COLS), COLS)


PHASES = ((0, 2 * CG), (2 * CG, CG), (3 * CG, CG))


def kernel(
    x_ref, w_ref, u_hbm, v_hbm, n_hbm, far_ids, ranks, near_ids, params, weights, counts,
    fwd, adj, grad,
    xo, wo, u_ref, v_ref, n_ref, ids, table, lists, prod, nprod, part, mate_in, mine, pass_in, done_in,
    side_out, side_in, sens, sgot, high_hot, low_hot, grid, got, row, ring,
    local, gsend, grecv, send, recv, ssend, srecv, psend, precv, csend, crecv,
):
    c, s, y, p, up, down, far = place()
    to_up, to_down = {"sub": 2 * up + p}, {"sub": 2 * down + p}
    to_mate = {"sub": 2 * y + 1 - p}
    to_next, to_prev = {"clus": (c + 1) % GROUPS}, {"clus": (c + GROUPS - 1) % GROUPS}
    barrier = pltpu.get_barrier_semaphore()

    def tell_sub(off, carry):
        pl.semaphore_signal(barrier, inc=1, device_id={"sub": (s + off) % MEMBERS}, device_id_type=MESH)
        return carry

    def tell_clus(off, carry):
        pl.semaphore_signal(barrier, inc=1, device_id={"clus": (c + off) % GROUPS}, device_id_type=MESH)
        return carry

    lax.fori_loop(1, MEMBERS, tell_sub, 0)
    lax.fori_loop(1, GROUPS, tell_clus, 0)

    own = pl.ds(CG, CG)
    keep = [
        pltpu.make_async_copy(w_ref, wo.at[:, :, cols(s)], local.at[0]),
        pltpu.make_async_copy(x_ref, xo.at[own, :, cols(s)], local.at[1]),
        pltpu.make_async_copy(u_hbm, u_ref, local.at[2]),
        pltpu.make_async_copy(v_hbm, v_ref, local.at[3]),
        pltpu.make_async_copy(n_hbm, n_ref, local.at[4]),
    ]
    for d in keep:
        d.start()

    first = c * CG
    total = GROUPS * CG
    big = 127
    ids[...] = jnp.full_like(ids, -1)
    ids[0:2, :] = far_ids[...]
    ids[2:4, 0:NEAR] = near_ids[...]
    sub_i = lax.broadcasted_iota(jnp.int32, (FAR, FAR), 0)
    lane_i = lax.broadcasted_iota(jnp.int32, (FAR, FAR), 1)
    slot_row = lax.broadcasted_iota(jnp.int32, (1, FAR), 1)
    table[...] = jnp.zeros_like(table)

    def order(key, payload, at, end_at, none):
        k = jnp.broadcast_to(key, (FAR, FAR))
        kt = k.T
        tie = (k == kt) & (lane_i < sub_i)
        ones = jnp.ones_like(k)
        zeros = jnp.zeros_like(k)
        rank = jnp.sum(jnp.where((k < kt) | tie, ones, zeros), axis=1, keepdims=True)
        opens = jnp.sum(jnp.where(tie, ones, zeros), axis=1, keepdims=True) == 0
        pay = jnp.broadcast_to(payload, (FAR, FAR)).T + jnp.where(opens, 1 << 20, 0)
        table[pl.ds(at, 1), :] = jnp.sum(jnp.where(rank == lane_i, pay, zeros), axis=0, keepdims=True)
        upto = jnp.sum(jnp.where(kt <= lane_i, ones, zeros), axis=0, keepdims=True)
        below = jnp.sum(jnp.where(kt < lane_i, ones, zeros), axis=0, keepdims=True)
        table[pl.ds(end_at, 1), :] = jnp.where(upto > below, upto - 1, none)

    for i, count in ((0, FAR), (1, NEAR)):
        live = slot_row < count
        r = jnp.clip(ids[2 * i : 2 * i + 1, :] - first, 0, CG - 1)
        q = jnp.clip((ids[2 * i + 1 : 2 * i + 2, :] - first + CG + total) % total, 0, 3 * CG - 1)
        payload = slot_row + q * 128 + r * 16384
        if i == 0:
            payload = payload + (ranks[...] << 21)
        order(jnp.where(live, q, big), payload, 2 * i, 5 + 2 * i, count)
        order(jnp.where(live, r, big), payload, 2 * i + 1, 6 + 2 * i, count)
    to_lists = pltpu.make_async_copy(table, lists, local.at[5])
    to_lists.start()


    devices = GROUPS * MEMBERS
    high = lax.broadcasted_iota(jnp.int32, (devices, CS), 0).astype(F32).astype(BF16)
    low = lax.broadcasted_iota(jnp.int32, (CS, CS), 0).astype(F32).astype(BF16)
    one, zero = jnp.ones((), BF16), jnp.zeros((), BF16)

    def hot(j, carry):
        at = pl.multiple_of((4 * s + j) * CS, CS)
        for m in range(4):
            q = params[pl.ds(m, 1), pl.ds(at, CS)]
            owner = q // CS
            owner = ((owner % MEMBERS) * GROUPS + owner // MEMBERS).astype(F32)
            below = (q % CS).astype(F32)
            here = pl.ds(pl.multiple_of((j % 2) * 4 * CS + m * CS, CS), CS)
            wide = jnp.broadcast_to(owner, (devices, CS)).astype(BF16)
            high_hot[j // 2, :, here] = jnp.where(high == wide, one, zero)
            low_hot[j // 2, :, here] = jnp.where(low == wide_of(below), one, zero)
        return carry

    def wide_of(v):
        return jnp.broadcast_to(v, (CS, CS)).astype(BF16)

    pl.semaphore_wait(barrier, MEMBERS - 1 + GROUPS - 1)

    subs = [2 * t + p for t in (y, down, up, far)]
    mates = [2 * t + 1 - p for t in (y, down, up, far)]
    started = []

    def gcopy(src, dst, k, peer):
        return pltpu.make_async_remote_copy(
            src_ref=src, dst_ref=dst, send_sem=gsend.at[k], recv_sem=grecv.at[k], device_id=peer, device_id_type=MESH
        )

    def ggo(src, dst, k, peer):
        d = gcopy(src, dst, k, peer)
        d.start()
        started.append(d)

    def garrived(ref, k):
        gcopy(ref, ref, k, to_mate).wait_recv()

    left_x, right_x = pl.ds(0, CG), pl.ds(2 * CG, CG)
    ggo(w_ref, wo.at[:, :, cols(s)], 0, to_up)
    ggo(w_ref, wo.at[:, :, cols(s)], 1, to_down)
    ggo(w_ref, wo.at[:, :, cols(s)], 14, to_mate)
    ggo(x_ref, xo.at[left_x, :, cols(s)], 6, to_next)
    ggo(x_ref, xo.at[right_x, :, cols(s)], 10, to_prev)
    ggo(x_ref, xo.at[own, :, cols(s)], 3, to_up)
    ggo(x_ref, xo.at[own, :, cols(s)], 4, to_down)
    ggo(x_ref, xo.at[own, :, cols(s)], 18, to_mate)

    def got_w(i):
        ref = wo.at[:, :, cols(subs[i])]
        garrived(ref, i - 1)
        if i == 2:
            ggo(ref, ref, 2, to_down)
        ggo(ref, ref, 14 + i, to_mate)

    def got_x(i):
        ref = xo.at[own, :, cols(subs[i])]
        garrived(ref, 2 + i)
        if i == 1:
            ggo(ref, ref, 5, to_up)
        ggo(ref, xo.at[left_x, :, cols(subs[i])], 6 + i, to_next)
        ggo(ref, xo.at[right_x, :, cols(subs[i])], 10 + i, to_prev)
        ggo(ref, ref, 18 + i, to_mate)

    def got_side(i):
        left = xo.at[left_x, :, cols(subs[i])]
        garrived(left, 6 + i)
        ggo(left, left, 22 + i, to_mate)
        right = xo.at[right_x, :, cols(subs[i])]
        garrived(right, 10 + i)
        ggo(right, right, 26 + i, to_mate)

    lax.fori_loop(0, 4, hot, 0)
    got_w(2)
    got_w(1)
    got_x(1)
    got_x(2)
    got_side(0)
    got_w(3)
    to_lists.wait()
    keep[0].wait()
    keep[2].wait()
    keep[3].wait()
    for i in range(4):
        garrived(wo.at[:, :, cols(mates[i])], 14 + i)

    xr, wr = xo, wo
    parts = part.reshape(WIDE, 2, MEMBERS * COLS, CS)
    lane = lax.broadcasted_iota(jnp.int32, (1, 256), 1)

    def decode(t):
        return t & 127, (t >> 7) & 127, (t >> 14) & 63, (1 - ((t >> 20) & 1)).astype(F32), t >> 21

    def far_inner(g, forward):
        got_t = [decode(lists[1 if forward else 0, 4 * g + i]) for i in range(4)]
        keepers = [((lane // 64 == i) & (lane % RANK < got_t[i][4])).astype(F32) for i in range(4)]
        if forward:
            src = jnp.concatenate([rows(xr, t[1], False) for t in got_t], axis=0)
            inner = jnp.concatenate([real_form(v_ref, t[0], -1) for t in got_t], axis=0)
        else:
            src = jnp.concatenate([rows(wr, t[2], True) for t in got_t], axis=0)
            inner = jnp.concatenate([real_form(u_ref, t[0], 1) for t in got_t], axis=0)
        m = mm(src, inner, NT)
        m = jnp.concatenate([(m[32 * i : 32 * i + 32] * keepers[i]).astype(BF16) for i in range(4)], axis=0)
        return m, got_t

    def far_outer(g, run, m, got_t, forward):
        if forward:
            outer = jnp.concatenate([real_form(u_ref, t[0], 1) for t in got_t], axis=0)
        else:
            outer = jnp.concatenate([real_form(v_ref, t[0], -1) for t in got_t], axis=0)
        z = mm(m, outer, NN)
        for i in range(4):
            run = z[32 * i : 32 * i + 32] + got_t[i][3] * run
            prod[4 * g + i] = run
        return run

    def near_block(i, run, forward):
        b, q, r, cont, _ = decode(lists[3 if forward else 2, i])
        nm = real_form(n_ref, b, -1)
        z = mm(rows(xr, q, False), nm, NT) if forward else mm(rows(wr, r, True), nm, NN)
        run = z + cont * run
        nprod[i] = run
        return run

    blank = jnp.zeros((MEMBERS * COLS, 2 * CS), F32)
    prod[FAR] = blank
    nprod[NEAR] = blank
    FU, NU = 8, 8

    def far_segment(seg, run, forward):
        n = FAR // 4 // SEGS // FU

        def step(i, run):
            at = [(seg * n + i) * FU + h for h in range(FU)]
            inner = [far_inner(g, forward) for g in at]
            for g, (m, got_t) in zip(at, inner):
                run = far_outer(g, run, m, got_t, forward)
            return run

        return lax.fori_loop(0, n, step, run)

    def near_all(forward):
        def step(i, run):
            for h in range(NU):
                run = near_block(i * NU + h, run, forward)
            return run

        lax.fori_loop(0, NEAR // NU, step, blank)

    def collect(lo, hi, shift, far_end, near_end):
        def step(i, carry):
            for h in range(4):
                k = lo + i * 4 + h
                a = prod[lists[far_end, k + shift]] + nprod[lists[near_end, k + shift]]
                parts[k, 0] = a[:, :CS]
                parts[k, 1] = a[:, CS:]
            return carry

        lax.fori_loop(0, (hi - lo) // 4, step, 0)

    run = far_segment(0, blank, False)
    got_x(3)
    far_segment(1, run, False)
    got_side(1)
    keep[4].wait()
    near_all(False)

    def copy(src, dst, k, peer):
        return pltpu.make_async_remote_copy(
            src_ref=src, dst_ref=dst, send_sem=send.at[k], recv_sem=recv.at[k], device_id=peer, device_id_type=MESH
        )

    def go(src, dst, k, peer):
        d = copy(src, dst, k, peer)
        d.start()
        started.append(d)

    def arrived(ref, k):
        copy(ref, ref, k, to_mate).wait_recv()

    tos = [far, up, down, y]
    chunk = 8

    def to_the_mate(ph):
        at = pl.ds(*PHASES[ph])
        for j in range(4):
            go(part.at[at, :, 2 * tos[j] + 1 - p], mate_in.at[j, at], 10 * ph + j, to_mate)

    def pair_sum(j, lo, n, extra=None):
        who = 2 * tos[j] + p

        def step(i, carry):
            at = pl.ds(lo + i * chunk, chunk)
            a = part[at, :, who] + mate_in[j, at]
            if extra is not None:
                a = a + pass_in[extra, at].astype(F32)
            mine[j, at] = a.astype(BF16)
            return carry

        lax.fori_loop(0, n // chunk, step, 0)

    def halves(ph):
        lo, n = PHASES[ph]
        n = n // 2
        return lo, lo + n, n, pl.ds(lo, n), pl.ds(lo + n, n), 10 * ph + 4

    def open_phase(ph):
        a, b, n, at_a, at_b, k = halves(ph)
        everything = pl.ds(*PHASES[ph])
        arrived(mate_in.at[0, everything], 10 * ph)
        pair_sum(0, a, n)
        go(mine.at[0, at_a], pass_in.at[0, at_a], k, to_up)
        pair_sum(0, b, n)
        go(mine.at[0, at_b], pass_in.at[1, at_b], k + 1, to_down)
        arrived(mate_in.at[1, everything], 10 * ph + 1)
        pair_sum(1, b, n)
        go(mine.at[1, at_b], done_in.at[0, at_b], k + 2, to_up)
        arrived(mate_in.at[2, everything], 10 * ph + 2)
        pair_sum(2, a, n)
        go(mine.at[2, at_a], done_in.at[1, at_a], k + 3, to_down)

    def pass_phase(ph):
        a, b, n, at_a, at_b, k = halves(ph)
        arrived(pass_in.at[0, at_a], k)
        pair_sum(1, a, n, 0)
        go(mine.at[1, at_a], done_in.at[0, at_a], k + 4, to_up)
        arrived(pass_in.at[1, at_b], k + 1)
        pair_sum(2, b, n, 1)
        go(mine.at[2, at_b], done_in.at[1, at_b], k + 5, to_down)

    def close_phase(ph):
        a, b, n, at_a, at_b, k = halves(ph)
        arrived(mate_in.at[3, pl.ds(*PHASES[ph])], 10 * ph + 3)
        arrived(done_in.at[0, at_b], k + 2)
        arrived(done_in.at[1, at_a], k + 3)
        arrived(done_in.at[0, at_a], k + 4)
        arrived(done_in.at[1, at_b], k + 5)

    def whole(at):
        a = part[at, :, s] + mate_in[3, at]
        return a + done_in[0, at].astype(F32) + done_in[1, at].astype(F32)

    collect(0, CG, 0, 5, 7)
    collect(CG, 2 * CG, CG, 5, 7)
    to_the_mate(0)
    got_side(2)
    collect(2 * CG, 3 * CG, -CG, 5, 7)
    to_the_mate(1)
    open_phase(0)
    got_side(3)
    open_phase(1)
    keep[1].wait()
    for i in range(4):
        garrived(xo.at[own, :, cols(mates[i])], 18 + i)
        garrived(xo.at[left_x, :, cols(mates[i])], 22 + i)
        garrived(xo.at[right_x, :, cols(mates[i])], 26 + i)

    run = far_segment(0, blank, True)
    pass_phase(0)
    far_segment(1, run, True)
    pass_phase(1)
    near_all(True)
    collect(3 * CG, 4 * CG, -3 * CG, 6, 8)
    to_the_mate(2)
    close_phase(0)

    def edge(i, carry):
        at = pl.ds(i * chunk, chunk)
        side_out[at] = whole(at)
        return carry

    lax.fori_loop(0, CG // chunk, edge, 0)
    go(side_out.at[pl.ds(0, CG)], side_in.at[0], 30, to_prev)
    lax.fori_loop(CG // chunk, 2 * CG // chunk, edge, 0)
    go(side_out.at[pl.ds(CG, CG)], side_in.at[1], 31, to_next)
    open_phase(2)
    close_phase(1)
    pass_phase(2)
    arrived(side_in.at[0], 30)
    arrived(side_in.at[1], 31)

    def own_adjoint(i, carry):
        at = i * chunk
        here = pl.ds(at, chunk)
        a = whole(pl.ds(2 * CG + at, chunk)) + side_in[0, here] + side_in[1, here]
        adj[here, 0] = a[:, 0]
        adj[here, 1] = -a[:, 1]
        return carry

    lax.fori_loop(0, CG // chunk, own_adjoint, 0)
    close_phase(2)

    def last(i, carry):
        here = pl.ds(i * chunk, chunk)
        f = whole(pl.ds(3 * CG + i * chunk, chunk))
        fwd[here] = f
        prd = f[:, 0] * adj[here, 0] - f[:, 1] * adj[here, 1]
        both = jnp.sum(prd, axis=1) * (1.0 / (MEMBERS * COLS))
        sens[2 * i] = both[:COLS]
        sens[2 * i + 1] = both[COLS:]
        return carry

    lax.fori_loop(0, CG // chunk, last, 0)

    sent = []

    def spread(src_of, dst, sems_out, sems_in):
        out = []
        for off in range(1, MEMBERS):
            to = (s + off) % MEMBERS
            d = pltpu.make_async_remote_copy(
                src_ref=src_of(to), dst_ref=dst.at[off - 1], send_sem=sems_out.at[off - 1],
                recv_sem=sems_in.at[off - 1], device_id={"sub": to}, device_id_type=MESH,
            )
            d.start()
            out.append(d)
        sent.extend(out)
        return out

    for d in spread(lambda to: sens.at[to], sgot, ssend, srecv):
        d.wait_recv()
    value = sens[s]
    for off in range(MEMBERS - 1):
        value = value + sgot[off]
    counted = counts[pl.ds(pl.multiple_of(4 * s, 4), 4), :]
    total_grid = None
    for k in range(2):
        tops, rests = [], []
        for h in range(2):
            j = 2 * k + h
            at = pl.multiple_of((4 * s + j) * CS, CS)
            for m in range(4):
                wt = weights[pl.ds(m, 1), pl.ds(at, CS)]
                val = wt * value[j : j + 1]
                val = jnp.where(counted[j : j + 1] > m, val, jnp.zeros_like(val))
                top = val.astype(BF16).astype(F32)
                lo = (4 * h + m) * CS
                here = low_hot[k, :, lo : lo + CS]
                tops.append(here * wide_of(top))
                rests.append(here * wide_of(val - top))
        hits = jnp.concatenate([jnp.concatenate(tops, axis=1), jnp.concatenate(rests, axis=1)], axis=0)
        g = mm(high_hot[k], hits, NT)
        g = g[:, :CS] + g[:, CS:]
        total_grid = g if k == 0 else total_grid + g
    grid[...] = total_grid

    def part_of(member):
        return grid.at[pl.ds(pl.multiple_of(member * GROUPS, GROUPS), GROUPS)]

    arrivals = spread(part_of, got, psend, precv)
    all_rows = grid[pl.ds(pl.multiple_of(s * GROUPS, GROUPS), GROUPS), :]
    for d in arrivals:
        d.wait_recv()
    for off in range(MEMBERS - 1):
        all_rows = all_rows + got[off]
    for k in range(GROUPS):
        row[k] = all_rows[k : k + 1]

    def ccopy(off):
        return pltpu.make_async_remote_copy(
            src_ref=row.at[(c + off) % GROUPS], dst_ref=ring.at[off - 1], send_sem=csend.at[off - 1],
            recv_sem=crecv.at[off - 1], device_id={"clus": (c + off) % GROUPS}, device_id_type=MESH,
        )

    def start(off, carry):
        ccopy(off).start()
        return carry

    def wait(off, carry):
        ccopy(off).wait()
        return carry

    lax.fori_loop(1, GROUPS, start, 0)
    for d in sent + started:
        d.wait_send()
    lax.fori_loop(1, GROUPS, wait, 0)
    final = row[c]
    for k in range(GROUPS - 1):
        final = final + ring[k]
    grad[...] = final


def hand_out(a, b, c, x, y, z):
    x[...] = a[...]
    y[...] = b[...]
    z[...] = c[...]


ANY = pl.BlockSpec(memory_space=pl.ANY)
VMEM = pl.BlockSpec(memory_space=pltpu.VMEM)


def split_form(x):
    n = x.shape[0]
    return x.reshape(n, COLS, 2, CS).transpose(0, 2, 1, 3)


def joined(x):
    n = x.shape[0]
    return x.transpose(0, 2, 1, 3).reshape(n, COLS, 2 * CS)


def shards(x, w, far_ids, ranks, far_left, far_right, near_ids, near, params, weights, counts):
    def sems(n):
        return pltpu.SemaphoreType.DMA((n,))

    half = (2, COLS, CS)
    fwd, adj, grad = pl.pallas_call(
        kernel,
        out_shape=(
            jax.ShapeDtypeStruct((CG,) + half, F32),
            jax.ShapeDtypeStruct((CG,) + half, F32),
            jax.ShapeDtypeStruct((1, CS), F32),
        ),
        in_specs=[ANY] * 5 + [VMEM] * 6,
        out_specs=(VMEM, VMEM, VMEM),
        scratch_shapes=[
            pltpu.VMEM((3 * CG, 2, MEMBERS * COLS, CS), BF16),
            pltpu.VMEM((CG, 2, MEMBERS * COLS, CS), BF16),
            pltpu.VMEM((FAR, 2, RANK, CS), BF16),
            pltpu.VMEM((FAR, 2, RANK, CS), BF16),
            pltpu.VMEM((NEAR, 2, CS, CS), BF16),
            pltpu.VMEM((8, FAR), jnp.int32),
            pltpu.VMEM((16, FAR), jnp.int32),
            pltpu.SMEM((16, FAR), jnp.int32),
            pltpu.VMEM((FAR + 1, MEMBERS * COLS, 2 * CS), F32),
            pltpu.VMEM((NEAR + 1, MEMBERS * COLS, 2 * CS), F32),
            pltpu.VMEM((WIDE, 2, MEMBERS, COLS, CS), F32),
            pltpu.VMEM((4, WIDE) + half, F32),
            pltpu.VMEM((3, WIDE) + half, BF16),
            pltpu.VMEM((2, WIDE) + half, BF16),
            pltpu.VMEM((2, WIDE) + half, BF16),
            pltpu.VMEM((2 * CG,) + half, F32),
            pltpu.VMEM((2, CG) + half, F32),
            pltpu.VMEM((MEMBERS, COLS, CS), F32),
            pltpu.VMEM((MEMBERS - 1, COLS, CS), F32),
            pltpu.VMEM((2, GROUPS * MEMBERS, 8 * CS), BF16),
            pltpu.VMEM((2, CS, 8 * CS), BF16),
            pltpu.VMEM((GROUPS * MEMBERS, CS), F32),
            pltpu.VMEM((MEMBERS - 1, GROUPS, CS), F32),
            pltpu.VMEM((GROUPS, 1, CS), F32),
            pltpu.VMEM((GROUPS - 1, 1, CS), F32),
            sems(6),
            sems(30),
            sems(30),
            sems(32),
            sems(32),
            sems(MEMBERS - 1),
            sems(MEMBERS - 1),
            sems(MEMBERS - 1),
            sems(MEMBERS - 1),
            sems(GROUPS - 1),
            sems(GROUPS - 1),
        ],
        compiler_params=pltpu.CompilerParams(collective_id=0, has_side_effects=True, vmem_limit_bytes=60 << 20),
        name="operator",
    )(
        split_form(x), split_form(w), far_left, far_right, near, far_ids, ranks.reshape(1, FAR), near_ids,
        params, weights, counts.reshape(CG, CS),
    )
    fwd, adj, grad = pl.pallas_call(
        hand_out,
        out_shape=tuple(jax.ShapeDtypeStruct(a.shape, a.dtype) for a in (fwd, adj, grad)),
        in_specs=[VMEM] * 3,
        out_specs=(VMEM,) * 3,
        name="hand_out",
    )(fwd, adj, grad)
    return joined(fwd), joined(adj), grad.reshape(CS)


def solution(mesh):
    rhs = P("clus", "sub", None)
    blocks = P(("clus", "sub"), None, None, None)
    both = ("clus", "sub")
    in_specs = (rhs, rhs, P(None, both), P(both), blocks, blocks, P(None, both), blocks)
    in_specs += (P(None, "clus"), P(None, "clus"), P("clus"))
    out_specs = (rhs, rhs, P(both))
    return jax.shard_map(shards, mesh=mesh, in_specs=in_specs, out_specs=out_specs, check_vma=False)
```

```python
import jax
import jax.numpy as jnp
from jax import lax
from jax.experimental import pallas as pl
from jax.experimental.pallas import tpu as pltpu
from jax.sharding import PartitionSpec as P

MESH = pl.DeviceIdType.MESH
F32 = jnp.float32
BF16 = jnp.bfloat16

GROUPS = 32
MEMBERS = 8
RING = 4
CG = 32
COLS = 4
CS = 128
RANK = 32
FAR = 128
NEAR = 32
SEGS = 2
WIDE = 4 * CG


def place():
    c = lax.axis_index("clus")
    s = lax.axis_index("sub")
    y = s // 2
    p = s % 2
    up, down, far = (y + 1) % RING, (y + 3) % RING, (y + 2) % RING
    return c, s, y, p, up, down, far


NT = (((1,), (1,)), ((), ()))
NN = (((1,), (0,)), ((), ()))


def mm(a, b, dims):
    return lax.dot_general(a, b, dims, preferred_element_type=F32)


def real_form(ref, b, sign):
    re, im = ref[b, 0], ref[b, 1]
    if sign > 0:
        top, low = [re, im], [-im, re]
    else:
        top, low = [re, -im], [im, re]
    return jnp.concatenate([jnp.concatenate(top, axis=1), jnp.concatenate(low, axis=1)], axis=0)


def rows(ref, r, conj):
    re, im = ref[r, 0], ref[r, 1]
    return jnp.concatenate([re, -im if conj else im], axis=1)


def cols(member):
    return pl.ds(pl.multiple_of(COLS * member, COLS), COLS)


PHASES = ((0, 2 * CG), (2 * CG, CG), (3 * CG, CG))


def kernel(
    x_ref, w_ref, u_hbm, v_hbm, n_hbm, far_ids, ranks, near_ids, params, weights, counts,
    fwd, adj, grad,
    xo, wo, u_ref, v_ref, n_ref, ids, table, lists, prod, nprod, part, mate_in, mine, pass_in, done_in,
    side_out, side_in, sens, sgot, summed, high_hot, low_hot, row, ring,
    local, gsend, grecv, send, recv, ssend, srecv, csend, crecv,
):
    c, s, y, p, up, down, far = place()
    to_up, to_down = {"sub": 2 * up + p}, {"sub": 2 * down + p}
    to_mate, to_far = {"sub": 2 * y + 1 - p}, {"sub": 2 * far + p}
    to_next, to_prev = {"clus": (c + 1) % GROUPS}, {"clus": (c + GROUPS - 1) % GROUPS}
    barrier = pltpu.get_barrier_semaphore()

    def tell_sub(off, carry):
        pl.semaphore_signal(barrier, inc=1, device_id={"sub": (s + off) % MEMBERS}, device_id_type=MESH)
        return carry

    def tell_clus(off, carry):
        pl.semaphore_signal(barrier, inc=1, device_id={"clus": (c + off) % GROUPS}, device_id_type=MESH)
        return carry

    lax.fori_loop(1, MEMBERS, tell_sub, 0)
    lax.fori_loop(1, GROUPS, tell_clus, 0)

    own = pl.ds(CG, CG)
    keep = [
        pltpu.make_async_copy(w_ref, wo.at[:, :, cols(s)], local.at[0]),
        pltpu.make_async_copy(x_ref, xo.at[own, :, cols(s)], local.at[1]),
        pltpu.make_async_copy(u_hbm, u_ref, local.at[2]),
        pltpu.make_async_copy(v_hbm, v_ref, local.at[3]),
        pltpu.make_async_copy(n_hbm, n_ref, local.at[4]),
    ]
    for d in keep:
        d.start()

    first = c * CG
    total = GROUPS * CG
    big = 127
    ids[...] = jnp.full_like(ids, -1)
    ids[0:2, :] = far_ids[...]
    ids[2:4, 0:NEAR] = near_ids[...]
    sub_i = lax.broadcasted_iota(jnp.int32, (FAR, FAR), 0)
    lane_i = lax.broadcasted_iota(jnp.int32, (FAR, FAR), 1)
    slot_row = lax.broadcasted_iota(jnp.int32, (1, FAR), 1)
    table[...] = jnp.zeros_like(table)

    def order(key, payload, at, end_at, none):
        k = jnp.broadcast_to(key, (FAR, FAR))
        kt = k.T
        tie = (k == kt) & (lane_i < sub_i)
        ones = jnp.ones_like(k)
        zeros = jnp.zeros_like(k)
        rank = jnp.sum(jnp.where((k < kt) | tie, ones, zeros), axis=1, keepdims=True)
        opens = jnp.sum(jnp.where(tie, ones, zeros), axis=1, keepdims=True) == 0
        pay = jnp.broadcast_to(payload, (FAR, FAR)).T + jnp.where(opens, 1 << 20, 0)
        table[pl.ds(at, 1), :] = jnp.sum(jnp.where(rank == lane_i, pay, zeros), axis=0, keepdims=True)
        upto = jnp.sum(jnp.where(kt <= lane_i, ones, zeros), axis=0, keepdims=True)
        below = jnp.sum(jnp.where(kt < lane_i, ones, zeros), axis=0, keepdims=True)
        table[pl.ds(end_at, 1), :] = jnp.where(upto > below, upto - 1, none)

    for i, count in ((0, FAR), (1, NEAR)):
        live = slot_row < count
        r = jnp.clip(ids[2 * i : 2 * i + 1, :] - first, 0, CG - 1)
        q = jnp.clip((ids[2 * i + 1 : 2 * i + 2, :] - first + CG + total) % total, 0, 3 * CG - 1)
        payload = slot_row + q * 128 + r * 16384
        if i == 0:
            payload = payload + (ranks[...] << 21)
        order(jnp.where(live, q, big), payload, 2 * i, 5 + 2 * i, count)
        order(jnp.where(live, r, big), payload, 2 * i + 1, 6 + 2 * i, count)
    to_lists = pltpu.make_async_copy(table, lists, local.at[5])
    to_lists.start()


    high = (lax.broadcasted_iota(jnp.int32, (GROUPS, CS), 0) * MEMBERS + s).astype(F32).astype(BF16)
    low = lax.broadcasted_iota(jnp.int32, (CS, CS), 0).astype(F32).astype(BF16)
    one, zero = jnp.ones((), BF16), jnp.zeros((), BF16)

    def hot(k, carry):
        at = pl.multiple_of(k * CS, CS)
        for m in range(4):
            q = params[pl.ds(m, 1), pl.ds(at, CS)]
            here = slice(m * CS, m * CS + CS)
            owner = (q // CS).astype(F32)
            high_hot[k, :, here] = jnp.where(high == wide_of(owner, GROUPS), one, zero)
            low_hot[k, :, here] = jnp.where(low == wide_of((q % CS).astype(F32), CS), one, zero)
        return carry

    def wide_of(v, n):
        return jnp.broadcast_to(v, (n, CS)).astype(BF16)

    pl.semaphore_wait(barrier, MEMBERS - 1 + GROUPS - 1)

    subs = [2 * t + p for t in (y, down, up, far)]
    mates = [2 * t + 1 - p for t in (y, down, up, far)]
    started = []

    def gcopy(src, dst, k, peer):
        return pltpu.make_async_remote_copy(
            src_ref=src, dst_ref=dst, send_sem=gsend.at[k], recv_sem=grecv.at[k], device_id=peer, device_id_type=MESH
        )

    def ggo(src, dst, k, peer):
        d = gcopy(src, dst, k, peer)
        d.start()
        started.append(d)

    def garrived(ref, k):
        gcopy(ref, ref, k, to_mate).wait_recv()

    left_x, right_x = pl.ds(0, CG), pl.ds(2 * CG, CG)
    ggo(w_ref, wo.at[:, :, cols(s)], 2, to_far)
    ggo(x_ref, xo.at[left_x, :, cols(s)], 6, to_next)
    ggo(x_ref, xo.at[right_x, :, cols(s)], 10, to_prev)
    ggo(x_ref, xo.at[own, :, cols(s)], 3, to_up)
    ggo(w_ref, wo.at[:, :, cols(s)], 1, to_down)
    ggo(w_ref, wo.at[:, :, cols(s)], 0, to_up)
    ggo(x_ref, xo.at[own, :, cols(s)], 4, to_down)
    ggo(w_ref, wo.at[:, :, cols(s)], 14, to_mate)
    ggo(x_ref, xo.at[own, :, cols(s)], 18, to_mate)

    def got_w(i):
        ref = wo.at[:, :, cols(subs[i])]
        garrived(ref, i - 1)
        ggo(ref, ref, 14 + i, to_mate)

    def got_x(i):
        ref = xo.at[own, :, cols(subs[i])]
        garrived(ref, 2 + i)
        if i == 1:
            ggo(ref, ref, 5, to_up)
        ggo(ref, xo.at[left_x, :, cols(subs[i])], 6 + i, to_next)
        ggo(ref, xo.at[right_x, :, cols(subs[i])], 10 + i, to_prev)
        ggo(ref, ref, 18 + i, to_mate)

    def got_side(i):
        left = xo.at[left_x, :, cols(subs[i])]
        garrived(left, 6 + i)
        ggo(left, left, 22 + i, to_mate)
        right = xo.at[right_x, :, cols(subs[i])]
        garrived(right, 10 + i)
        ggo(right, right, 26 + i, to_mate)

    lax.fori_loop(0, 3 * CG // 4, hot, 0)
    got_side(0)
    lax.fori_loop(3 * CG // 4, CG, hot, 0)
    got_x(1)
    got_w(2)
    got_w(3)
    got_x(2)
    got_w(1)
    to_lists.wait()
    keep[0].wait()
    keep[2].wait()
    keep[3].wait()
    for i in range(4):
        garrived(wo.at[:, :, cols(mates[i])], 14 + i)

    xr, wr = xo, wo
    parts = part.reshape(WIDE, 2, MEMBERS * COLS, CS)
    lane = lax.broadcasted_iota(jnp.int32, (1, 256), 1)

    def decode(t):
        return t & 127, (t >> 7) & 127, (t >> 14) & 63, (1 - ((t >> 20) & 1)).astype(F32), t >> 21

    def far_inner(g, forward):
        got_t = [decode(lists[1 if forward else 0, 4 * g + i]) for i in range(4)]
        keepers = [((lane // 64 == i) & (lane % RANK < got_t[i][4])).astype(F32) for i in range(4)]
        if forward:
            src = jnp.concatenate([rows(xr, t[1], False) for t in got_t], axis=0)
            inner = jnp.concatenate([real_form(v_ref, t[0], -1) for t in got_t], axis=0)
        else:
            src = jnp.concatenate([rows(wr, t[2], True) for t in got_t], axis=0)
            inner = jnp.concatenate([real_form(u_ref, t[0], 1) for t in got_t], axis=0)
        m = mm(src, inner, NT)
        m = jnp.concatenate([(m[32 * i : 32 * i + 32] * keepers[i]).astype(BF16) for i in range(4)], axis=0)
        return m, got_t

    def far_outer(g, run, m, got_t, forward):
        if forward:
            outer = jnp.concatenate([real_form(u_ref, t[0], 1) for t in got_t], axis=0)
        else:
            outer = jnp.concatenate([real_form(v_ref, t[0], -1) for t in got_t], axis=0)
        z = mm(m, outer, NN)
        for i in range(4):
            run = z[32 * i : 32 * i + 32] + got_t[i][3] * run
            prod[4 * g + i] = run
        return run

    def near_product(i, forward):
        b, q, r, cont, _ = decode(lists[3 if forward else 2, i])
        nm = real_form(n_ref, b, -1)
        return (mm(rows(xr, q, False), nm, NT) if forward else mm(rows(wr, r, True), nm, NN)), cont

    blank = jnp.zeros((MEMBERS * COLS, 2 * CS), F32)
    prod[FAR] = blank
    nprod[NEAR] = blank
    FU, NU = 8, 8

    def far_segment(seg, run, forward):
        n = FAR // 4 // SEGS // FU

        def step(i, run):
            at = [(seg * n + i) * FU + h for h in range(FU)]
            inner = [far_inner(g, forward) for g in at]
            for g, (m, got_t) in zip(at, inner):
                run = far_outer(g, run, m, got_t, forward)
            return run

        return lax.fori_loop(0, n, step, run)

    def near_all(forward):
        def step(i, run):
            made = [near_product(i * NU + h, forward) for h in range(NU)]
            for h, (z, cont) in enumerate(made):
                run = z + cont * run
                nprod[i * NU + h] = run
            return run

        lax.fori_loop(0, NEAR // NU, step, blank)

    def collect(lo, hi, shift, far_end, near_end):
        def step(i, carry):
            for h in range(4):
                k = lo + i * 4 + h
                a = prod[lists[far_end, k + shift]] + nprod[lists[near_end, k + shift]]
                parts[k, 0] = a[:, :CS]
                parts[k, 1] = a[:, CS:]
            return carry

        lax.fori_loop(0, (hi - lo) // 4, step, 0)

    run = far_segment(0, blank, False)
    got_x(3)
    got_side(1)
    far_segment(1, run, False)
    got_side(2)
    keep[4].wait()
    near_all(False)
    got_side(3)

    def copy(src, dst, k, peer):
        return pltpu.make_async_remote_copy(
            src_ref=src, dst_ref=dst, send_sem=send.at[k], recv_sem=recv.at[k], device_id=peer, device_id_type=MESH
        )

    def go(src, dst, k, peer):
        d = copy(src, dst, k, peer)
        d.start()
        started.append(d)

    def arrived(ref, k):
        copy(ref, ref, k, to_mate).wait_recv()

    tos = [far, up, down, y]
    chunk = 8

    def to_the_mate(ph):
        at = pl.ds(*PHASES[ph])
        for j in range(4):
            go(part.at[at, :, 2 * tos[j] + 1 - p], mate_in.at[j, at], 10 * ph + j, to_mate)

    def pair_sum(j, lo, n, extra=None):
        who = 2 * tos[j] + p

        def step(i, carry):
            at = pl.ds(lo + i * chunk, chunk)
            a = part[at, :, who] + mate_in[j, at]
            if extra is not None:
                a = a + pass_in[extra, at].astype(F32)
            mine[j, at] = a.astype(BF16)
            return carry

        lax.fori_loop(0, n // chunk, step, 0)

    def halves(ph):
        lo, n = PHASES[ph]
        n = n // 2
        return lo, lo + n, n, pl.ds(lo, n), pl.ds(lo + n, n), 10 * ph + 4

    def open_phase(ph):
        a, b, n, at_a, at_b, k = halves(ph)
        everything = pl.ds(*PHASES[ph])
        arrived(mate_in.at[0, everything], 10 * ph)
        pair_sum(0, a, n)
        go(mine.at[0, at_a], pass_in.at[0, at_a], k, to_up)
        pair_sum(0, b, n)
        go(mine.at[0, at_b], pass_in.at[1, at_b], k + 1, to_down)
        arrived(mate_in.at[1, everything], 10 * ph + 1)
        pair_sum(1, b, n)
        go(mine.at[1, at_b], done_in.at[0, at_b], k + 2, to_up)
        arrived(mate_in.at[2, everything], 10 * ph + 2)
        pair_sum(2, a, n)
        go(mine.at[2, at_a], done_in.at[1, at_a], k + 3, to_down)

    def pass_phase(ph):
        a, b, n, at_a, at_b, k = halves(ph)
        arrived(pass_in.at[0, at_a], k)
        pair_sum(1, a, n, 0)
        go(mine.at[1, at_a], done_in.at[0, at_a], k + 4, to_up)
        arrived(pass_in.at[1, at_b], k + 1)
        pair_sum(2, b, n, 1)
        go(mine.at[2, at_b], done_in.at[1, at_b], k + 5, to_down)

    def direct_phase(ph):
        lo, n = PHASES[ph]
        at = pl.ds(lo, n)
        for j, peer, slot in ((0, to_far, 2), (1, to_up, 0), (2, to_down, 1)):
            arrived(mate_in.at[j, at], 10 * ph + j)
            pair_sum(j, lo, n)
            go(mine.at[j, at], done_in.at[slot, at], 10 * ph + 4 + j, peer)

    def close_direct(ph):
        at = pl.ds(*PHASES[ph])
        arrived(mate_in.at[3, at], 10 * ph + 3)
        for j, slot in ((0, 2), (1, 0), (2, 1)):
            arrived(done_in.at[slot, at], 10 * ph + 4 + j)

    def close_phase(ph):
        a, b, n, at_a, at_b, k = halves(ph)
        arrived(mate_in.at[3, pl.ds(*PHASES[ph])], 10 * ph + 3)
        arrived(done_in.at[0, at_b], k + 2)
        arrived(done_in.at[1, at_a], k + 3)
        arrived(done_in.at[0, at_a], k + 4)
        arrived(done_in.at[1, at_b], k + 5)

    def whole(at):
        a = part[at, :, s] + mate_in[3, at]
        return a + done_in[0, at].astype(F32) + done_in[1, at].astype(F32)

    collect(0, CG, 0, 5, 7)
    collect(CG, 2 * CG, CG, 5, 7)
    to_the_mate(0)
    collect(2 * CG, 3 * CG, -CG, 5, 7)
    to_the_mate(1)
    keep[1].wait()
    for i in range(4):
        garrived(xo.at[own, :, cols(mates[i])], 18 + i)
        garrived(xo.at[left_x, :, cols(mates[i])], 22 + i)
        garrived(xo.at[right_x, :, cols(mates[i])], 26 + i)
    open_phase(0)
    run = far_segment(0, blank, True)
    open_phase(1)
    far_segment(1, run, True)
    pass_phase(0)
    near_all(True)
    pass_phase(1)
    collect(3 * CG, 4 * CG, -3 * CG, 6, 8)
    to_the_mate(2)
    direct_phase(2)
    close_phase(0)

    def edge(i, carry):
        at = pl.ds(i * chunk, chunk)
        side_out[at] = whole(at).astype(BF16)
        return carry

    lax.fori_loop(0, CG // chunk, edge, 0)
    go(side_out.at[pl.ds(0, CG)], side_in.at[0], 30, to_prev)
    lax.fori_loop(CG // chunk, 2 * CG // chunk, edge, 0)
    go(side_out.at[pl.ds(CG, CG)], side_in.at[1], 31, to_next)
    close_phase(1)
    arrived(side_in.at[0], 30)
    arrived(side_in.at[1], 31)

    def own_adjoint(i, carry):
        at = i * chunk
        here = pl.ds(at, chunk)
        a = whole(pl.ds(2 * CG + at, chunk)) + side_in[0, here].astype(F32) + side_in[1, here].astype(F32)
        adj[here, 0] = a[:, 0]
        adj[here, 1] = -a[:, 1]
        return carry

    lax.fori_loop(0, CG // chunk, own_adjoint, 0)
    close_direct(2)

    def last(i, carry):
        here = pl.ds(i * chunk, chunk)
        at = pl.ds(3 * CG + i * chunk, chunk)
        f = whole(at) + done_in[2, at].astype(F32)
        fwd[here] = f
        prd = f[:, 0] * adj[here, 0] - f[:, 1] * adj[here, 1]
        sens[here] = jnp.sum(prd, axis=1) * (1.0 / (MEMBERS * COLS))
        return carry

    lax.fori_loop(0, CG // chunk, last, 0)

    sent = []
    for off in range(1, MEMBERS):
        d = pltpu.make_async_remote_copy(
            src_ref=sens, dst_ref=sgot.at[off - 1], send_sem=ssend.at[off - 1], recv_sem=srecv.at[off - 1],
            device_id={"sub": (s + off) % MEMBERS}, device_id_type=MESH,
        )
        d.start()
        sent.append(d)
    for d in sent:
        d.wait_recv()
    value = sens[...]
    for off in range(MEMBERS - 1):
        value = value + sgot[off]
    summed[...] = value
    KU = 4

    def clusters(i, acc):
        lhs = []
        for h in range(KU):
            k = i * KU + h
            at = pl.multiple_of(k * CS, CS)
            value, count = summed[pl.ds(k, 1), :], counts[pl.ds(k, 1), :]
            tops, rests = [], []
            for m in range(4):
                val = weights[pl.ds(m, 1), pl.ds(at, CS)] * value
                val = jnp.where(count > m, val, jnp.zeros_like(val))
                top = val.astype(BF16).astype(F32)
                hit = high_hot[k, :, m * CS : m * CS + CS]
                tops.append(hit * wide_of(top, GROUPS))
                rests.append(hit * wide_of(val - top, GROUPS))
            lhs.append(jnp.concatenate([jnp.concatenate(tops, axis=1), jnp.concatenate(rests, axis=1)], axis=0))
        made = [mm(lhs[h], low_hot[i * KU + h], NT) for h in range(KU)]
        for g in made:
            acc = acc + g
        return acc

    both = lax.fori_loop(0, CG // KU, clusters, jnp.zeros((2 * GROUPS, CS), F32))
    all_rows = both[:GROUPS] + both[GROUPS:]
    for k in range(GROUPS):
        row[k] = all_rows[k : k + 1]

    def ccopy(off):
        return pltpu.make_async_remote_copy(
            src_ref=row.at[(c + off) % GROUPS], dst_ref=ring.at[off - 1], send_sem=csend.at[off - 1],
            recv_sem=crecv.at[off - 1], device_id={"clus": (c + off) % GROUPS}, device_id_type=MESH,
        )

    def start(off, carry):
        ccopy(off).start()
        return carry

    def wait(off, carry):
        ccopy(off).wait()
        return carry

    lax.fori_loop(1, GROUPS, start, 0)
    for d in sent + started:
        d.wait_send()
    lax.fori_loop(1, GROUPS, wait, 0)
    final = row[c]
    for k in range(GROUPS - 1):
        final = final + ring[k]
    grad[...] = final


def hand_out(a, b, c, x, y, z):
    x[...] = a[...]
    y[...] = b[...]
    z[...] = c[...]


ANY = pl.BlockSpec(memory_space=pl.ANY)
VMEM = pl.BlockSpec(memory_space=pltpu.VMEM)


def split_form(x):
    n = x.shape[0]
    return x.reshape(n, COLS, 2, CS).transpose(0, 2, 1, 3)


def joined(x):
    n = x.shape[0]
    return x.transpose(0, 2, 1, 3).reshape(n, COLS, 2 * CS)


def shards(x, w, far_ids, ranks, far_left, far_right, near_ids, near, params, weights, counts):
    def sems(n):
        return pltpu.SemaphoreType.DMA((n,))

    half = (2, COLS, CS)
    fwd, adj, grad = pl.pallas_call(
        kernel,
        out_shape=(
            jax.ShapeDtypeStruct((CG,) + half, F32),
            jax.ShapeDtypeStruct((CG,) + half, F32),
            jax.ShapeDtypeStruct((1, CS), F32),
        ),
        in_specs=[ANY] * 5 + [VMEM] * 6,
        out_specs=(VMEM, VMEM, VMEM),
        scratch_shapes=[
            pltpu.VMEM((3 * CG, 2, MEMBERS * COLS, CS), BF16),
            pltpu.VMEM((CG, 2, MEMBERS * COLS, CS), BF16),
            pltpu.VMEM((FAR, 2, RANK, CS), BF16),
            pltpu.VMEM((FAR, 2, RANK, CS), BF16),
            pltpu.VMEM((NEAR, 2, CS, CS), BF16),
            pltpu.VMEM((8, FAR), jnp.int32),
            pltpu.VMEM((16, FAR), jnp.int32),
            pltpu.SMEM((16, FAR), jnp.int32),
            pltpu.VMEM((FAR + 1, MEMBERS * COLS, 2 * CS), F32),
            pltpu.VMEM((NEAR + 1, MEMBERS * COLS, 2 * CS), F32),
            pltpu.VMEM((WIDE, 2, MEMBERS, COLS, CS), F32),
            pltpu.VMEM((4, WIDE) + half, F32),
            pltpu.VMEM((3, WIDE) + half, BF16),
            pltpu.VMEM((2, WIDE) + half, BF16),
            pltpu.VMEM((3, WIDE) + half, BF16),
            pltpu.VMEM((2 * CG,) + half, BF16),
            pltpu.VMEM((2, CG) + half, BF16),
            pltpu.VMEM((CG, CS), F32),
            pltpu.VMEM((MEMBERS - 1, CG, CS), F32),
            pltpu.VMEM((CG, CS), F32),
            pltpu.VMEM((CG, GROUPS, 4 * CS), BF16),
            pltpu.VMEM((CG, CS, 4 * CS), BF16),
            pltpu.VMEM((GROUPS, 1, CS), F32),
            pltpu.VMEM((GROUPS - 1, 1, CS), F32),
            sems(6),
            sems(30),
            sems(30),
            sems(32),
            sems(32),
            sems(MEMBERS - 1),
            sems(MEMBERS - 1),
            sems(GROUPS - 1),
            sems(GROUPS - 1),
        ],
        compiler_params=pltpu.CompilerParams(collective_id=0, has_side_effects=True, vmem_limit_bytes=60 << 20),
        name="operator",
    )(
        split_form(x), split_form(w), far_left, far_right, near, far_ids, ranks.reshape(1, FAR), near_ids,
        params, weights, counts.reshape(CG, CS),
    )
    fwd, adj, grad = pl.pallas_call(
        hand_out,
        out_shape=tuple(jax.ShapeDtypeStruct(a.shape, a.dtype) for a in (fwd, adj, grad)),
        in_specs=[VMEM] * 3,
        out_specs=(VMEM,) * 3,
        name="hand_out",
    )(fwd, adj, grad)
    return joined(fwd), joined(adj), grad.reshape(CS)


def solution(mesh):
    rhs = P("clus", "sub", None)
    blocks = P(("clus", "sub"), None, None, None)
    both = ("clus", "sub")
    in_specs = (rhs, rhs, P(None, both), P(both), blocks, blocks, P(None, both), blocks)
    in_specs += (P(None, "clus"), P(None, "clus"), P("clus"))
    out_specs = (rhs, rhs, P(both))
    return jax.shard_map(shards, mesh=mesh, in_specs=in_specs, out_specs=out_specs, check_vma=False)
```

```python
import jax
import jax.numpy as jnp
from jax import lax
from jax.experimental import pallas as pl
from jax.experimental.pallas import tpu as pltpu
from jax.sharding import PartitionSpec as P

MESH = pl.DeviceIdType.MESH
F32 = jnp.float32
BF16 = jnp.bfloat16

GROUPS = 32
MEMBERS = 8
RING = 4
CG = 32
COLS = 4
CS = 128
RANK = 32
FAR = 128
NEAR = 32
SEGS = 2
WIDE = 4 * CG


def place():
    c = lax.axis_index("clus")
    s = lax.axis_index("sub")
    y = s // 2
    p = s % 2
    up, down, far = (y + 1) % RING, (y + 3) % RING, (y + 2) % RING
    return c, s, y, p, up, down, far


NT = (((1,), (1,)), ((), ()))
NN = (((1,), (0,)), ((), ()))


def mm(a, b, dims):
    return lax.dot_general(a, b, dims, preferred_element_type=F32)


def real_form(ref, b, sign):
    re, im = ref[b, 0], ref[b, 1]
    if sign > 0:
        top, low = [re, im], [-im, re]
    else:
        top, low = [re, -im], [im, re]
    return jnp.concatenate([jnp.concatenate(top, axis=1), jnp.concatenate(low, axis=1)], axis=0)


def rows(ref, r, conj):
    re, im = ref[r, 0], ref[r, 1]
    return jnp.concatenate([re, -im if conj else im], axis=1)


def cols(member):
    return pl.ds(pl.multiple_of(COLS * member, COLS), COLS)


PHASES = ((0, CG), (CG, CG), (2 * CG, CG), (3 * CG, CG))


def kernel(
    x_ref, w_ref, u_hbm, v_hbm, n_hbm, far_ids, ranks, near_ids, params, weights, counts,
    fwd, adj, grad,
    xo, wo, u_ref, v_ref, n_ref, ids, table, lists, prod, nprod, part, mate_in, mine, pass_in, done_in,
    side_out, side_in, sens, sgot, summed, high_hot, low_hot, row, ring,
    local, gsend, grecv, send, recv, ssend, srecv, csend, crecv,
):
    c, s, y, p, up, down, far = place()
    to_up, to_down = {"sub": 2 * up + p}, {"sub": 2 * down + p}
    to_mate, to_far = {"sub": 2 * y + 1 - p}, {"sub": 2 * far + p}
    to_next, to_prev = {"clus": (c + 1) % GROUPS}, {"clus": (c + GROUPS - 1) % GROUPS}
    barrier = pltpu.get_barrier_semaphore()

    def tell_sub(off, carry):
        pl.semaphore_signal(barrier, inc=1, device_id={"sub": (s + off) % MEMBERS}, device_id_type=MESH)
        return carry

    def tell_clus(off, carry):
        pl.semaphore_signal(barrier, inc=1, device_id={"clus": (c + off) % GROUPS}, device_id_type=MESH)
        return carry

    lax.fori_loop(1, MEMBERS, tell_sub, 0)
    lax.fori_loop(1, GROUPS, tell_clus, 0)

    own = pl.ds(CG, CG)
    keep = [
        pltpu.make_async_copy(w_ref, wo.at[:, :, cols(s)], local.at[0]),
        pltpu.make_async_copy(x_ref, xo.at[own, :, cols(s)], local.at[1]),
        pltpu.make_async_copy(u_hbm, u_ref, local.at[2]),
        pltpu.make_async_copy(v_hbm, v_ref, local.at[3]),
        pltpu.make_async_copy(n_hbm, n_ref, local.at[4]),
    ]
    for d in keep:
        d.start()

    first = c * CG
    total = GROUPS * CG
    big = 127
    ids[...] = jnp.full_like(ids, -1)
    ids[0:2, :] = far_ids[...]
    ids[2:4, 0:NEAR] = near_ids[...]
    sub_i = lax.broadcasted_iota(jnp.int32, (FAR, FAR), 0)
    lane_i = lax.broadcasted_iota(jnp.int32, (FAR, FAR), 1)
    slot_row = lax.broadcasted_iota(jnp.int32, (1, FAR), 1)
    table[...] = jnp.zeros_like(table)

    def order(key, payload, at, end_at, none):
        k = jnp.broadcast_to(key, (FAR, FAR))
        kt = k.T
        tie = (k == kt) & (lane_i < sub_i)
        ones = jnp.ones_like(k)
        zeros = jnp.zeros_like(k)
        rank = jnp.sum(jnp.where((k < kt) | tie, ones, zeros), axis=1, keepdims=True)
        opens = jnp.sum(jnp.where(tie, ones, zeros), axis=1, keepdims=True) == 0
        pay = jnp.broadcast_to(payload, (FAR, FAR)).T + jnp.where(opens, 1 << 20, 0)
        table[pl.ds(at, 1), :] = jnp.sum(jnp.where(rank == lane_i, pay, zeros), axis=0, keepdims=True)
        upto = jnp.sum(jnp.where(kt <= lane_i, ones, zeros), axis=0, keepdims=True)
        below = jnp.sum(jnp.where(kt < lane_i, ones, zeros), axis=0, keepdims=True)
        table[pl.ds(end_at, 1), :] = jnp.where(upto > below, upto - 1, none)

    for i, count in ((0, FAR), (1, NEAR)):
        live = slot_row < count
        r = jnp.clip(ids[2 * i : 2 * i + 1, :] - first, 0, CG - 1)
        q = jnp.clip((ids[2 * i + 1 : 2 * i + 2, :] - first + CG + total) % total, 0, 3 * CG - 1)
        payload = slot_row + q * 128 + r * 16384
        if i == 0:
            payload = payload + (ranks[...] << 21)
        order(jnp.where(live, q, big), payload, 2 * i, 5 + 2 * i, count)
        order(jnp.where(live, r, big), payload, 2 * i + 1, 6 + 2 * i, count)
    to_lists = pltpu.make_async_copy(table, lists, local.at[5])
    to_lists.start()


    high = (lax.broadcasted_iota(jnp.int32, (GROUPS, CS), 0) * MEMBERS + s).astype(F32).astype(BF16)
    low = lax.broadcasted_iota(jnp.int32, (CS, CS), 0).astype(F32).astype(BF16)
    one, zero = jnp.ones((), BF16), jnp.zeros((), BF16)

    def hot(k, carry):
        at = pl.multiple_of(k * CS, CS)
        for m in range(4):
            q = params[pl.ds(m, 1), pl.ds(at, CS)]
            here = slice(m * CS, m * CS + CS)
            owner = (q // CS).astype(F32)
            high_hot[k, :, here] = jnp.where(high == wide_of(owner, GROUPS), one, zero)
            low_hot[k, :, here] = jnp.where(low == wide_of((q % CS).astype(F32), CS), one, zero)
        return carry

    def wide_of(v, n):
        return jnp.broadcast_to(v, (n, CS)).astype(BF16)

    pl.semaphore_wait(barrier, MEMBERS - 1 + GROUPS - 1)

    subs = [2 * t + p for t in (y, down, up, far)]
    mates = [2 * t + 1 - p for t in (y, down, up, far)]
    started = []

    def gcopy(src, dst, k, peer):
        return pltpu.make_async_remote_copy(
            src_ref=src, dst_ref=dst, send_sem=gsend.at[k], recv_sem=grecv.at[k], device_id=peer, device_id_type=MESH
        )

    def ggo(src, dst, k, peer):
        d = gcopy(src, dst, k, peer)
        d.start()
        started.append(d)

    def garrived(ref, k):
        gcopy(ref, ref, k, to_mate).wait_recv()

    left_x, right_x = pl.ds(0, CG), pl.ds(2 * CG, CG)
    ggo(w_ref, wo.at[:, :, cols(s)], 2, to_far)
    ggo(x_ref, xo.at[left_x, :, cols(s)], 6, to_next)
    ggo(x_ref, xo.at[right_x, :, cols(s)], 10, to_prev)
    ggo(x_ref, xo.at[own, :, cols(s)], 3, to_up)
    ggo(w_ref, wo.at[:, :, cols(s)], 1, to_down)
    ggo(w_ref, wo.at[:, :, cols(s)], 0, to_up)
    ggo(x_ref, xo.at[own, :, cols(s)], 4, to_down)
    ggo(w_ref, wo.at[:, :, cols(s)], 14, to_mate)
    ggo(x_ref, xo.at[own, :, cols(s)], 18, to_mate)

    def got_w(i):
        ref = wo.at[:, :, cols(subs[i])]
        garrived(ref, i - 1)
        ggo(ref, ref, 14 + i, to_mate)

    def got_x(i):
        ref = xo.at[own, :, cols(subs[i])]
        garrived(ref, 2 + i)
        if i == 1:
            ggo(ref, ref, 5, to_up)
        ggo(ref, xo.at[left_x, :, cols(subs[i])], 6 + i, to_next)
        ggo(ref, xo.at[right_x, :, cols(subs[i])], 10 + i, to_prev)
        ggo(ref, ref, 18 + i, to_mate)

    def got_side(i):
        left = xo.at[left_x, :, cols(subs[i])]
        garrived(left, 6 + i)
        ggo(left, left, 22 + i, to_mate)
        right = xo.at[right_x, :, cols(subs[i])]
        garrived(right, 10 + i)
        ggo(right, right, 26 + i, to_mate)

    lax.fori_loop(0, 3 * CG // 4, hot, 0)
    got_side(0)
    lax.fori_loop(3 * CG // 4, CG, hot, 0)
    got_x(1)
    got_w(2)
    got_w(3)
    got_x(2)
    got_w(1)
    to_lists.wait()
    keep[0].wait()
    keep[2].wait()
    keep[3].wait()
    for i in range(4):
        garrived(wo.at[:, :, cols(mates[i])], 14 + i)

    xr, wr = xo, wo
    parts = part.reshape(WIDE, 2, MEMBERS * COLS, CS)
    lane = lax.broadcasted_iota(jnp.int32, (1, 256), 1)

    def decode(t):
        return t & 127, (t >> 7) & 127, (t >> 14) & 63, (1 - ((t >> 20) & 1)).astype(F32), t >> 21

    def far_inner(g, forward):
        got_t = [decode(lists[1 if forward else 0, 4 * g + i]) for i in range(4)]
        keepers = [((lane // 64 == i) & (lane % RANK < got_t[i][4])).astype(F32) for i in range(4)]
        if forward:
            src = jnp.concatenate([rows(xr, t[1], False) for t in got_t], axis=0)
            inner = jnp.concatenate([real_form(v_ref, t[0], -1) for t in got_t], axis=0)
        else:
            src = jnp.concatenate([rows(wr, t[2], True) for t in got_t], axis=0)
            inner = jnp.concatenate([real_form(u_ref, t[0], 1) for t in got_t], axis=0)
        m = mm(src, inner, NT)
        m = jnp.concatenate([(m[32 * i : 32 * i + 32] * keepers[i]).astype(BF16) for i in range(4)], axis=0)
        return m, got_t

    def far_outer(g, run, m, got_t, forward):
        if forward:
            outer = jnp.concatenate([real_form(u_ref, t[0], 1) for t in got_t], axis=0)
        else:
            outer = jnp.concatenate([real_form(v_ref, t[0], -1) for t in got_t], axis=0)
        z = mm(m, outer, NN)
        for i in range(4):
            run = z[32 * i : 32 * i + 32] + got_t[i][3] * run
            prod[4 * g + i] = run
        return run

    def near_product(i, forward):
        b, q, r, cont, _ = decode(lists[3 if forward else 2, i])
        nm = real_form(n_ref, b, -1)
        return (mm(rows(xr, q, False), nm, NT) if forward else mm(rows(wr, r, True), nm, NN)), cont

    blank = jnp.zeros((MEMBERS * COLS, 2 * CS), F32)
    prod[FAR] = blank
    nprod[NEAR] = blank
    FU, NU = 8, 8

    def far_segment(seg, run, forward):
        n = FAR // 4 // SEGS // FU

        def step(i, run):
            at = [(seg * n + i) * FU + h for h in range(FU)]
            inner = [far_inner(g, forward) for g in at]
            for g, (m, got_t) in zip(at, inner):
                run = far_outer(g, run, m, got_t, forward)
            return run

        return lax.fori_loop(0, n, step, run)

    def near_all(forward):
        def step(i, run):
            made = [near_product(i * NU + h, forward) for h in range(NU)]
            for h, (z, cont) in enumerate(made):
                run = z + cont * run
                nprod[i * NU + h] = run
            return run

        lax.fori_loop(0, NEAR // NU, step, blank)

    def collect(lo, hi, shift, far_end, near_end):
        def step(i, carry):
            for h in range(4):
                k = lo + i * 4 + h
                a = prod[lists[far_end, k + shift]] + nprod[lists[near_end, k + shift]]
                parts[k, 0] = a[:, :CS]
                parts[k, 1] = a[:, CS:]
            return carry

        lax.fori_loop(0, (hi - lo) // 4, step, 0)

    run = far_segment(0, blank, False)
    got_x(3)
    got_side(1)
    far_segment(1, run, False)
    got_side(2)
    keep[4].wait()
    near_all(False)
    got_side(3)

    def copy(src, dst, k, peer):
        return pltpu.make_async_remote_copy(
            src_ref=src, dst_ref=dst, send_sem=send.at[k], recv_sem=recv.at[k], device_id=peer, device_id_type=MESH
        )

    def go(src, dst, k, peer):
        d = copy(src, dst, k, peer)
        d.start()
        started.append(d)

    def arrived(ref, k):
        copy(ref, ref, k, to_mate).wait_recv()

    tos = [far, up, down, y]
    chunk = 8

    def to_the_mate(ph):
        at = pl.ds(*PHASES[ph])
        for j in range(4):
            go(part.at[at, :, 2 * tos[j] + 1 - p], mate_in.at[j, at], 10 * ph + j, to_mate)

    def pair_sum(j, lo, n, extra=None):
        who = 2 * tos[j] + p

        def step(i, carry):
            at = pl.ds(lo + i * chunk, chunk)
            a = part[at, :, who] + mate_in[j, at]
            if extra is not None:
                a = a + pass_in[extra, at].astype(F32)
            mine[j, at] = a.astype(BF16)
            return carry

        lax.fori_loop(0, n // chunk, step, 0)

    def halves(ph):
        lo, n = PHASES[ph]
        n = n // 2
        return lo, lo + n, n, pl.ds(lo, n), pl.ds(lo + n, n), 10 * ph + 4

    def open_phase(ph):
        a, b, n, at_a, at_b, k = halves(ph)
        everything = pl.ds(*PHASES[ph])
        arrived(mate_in.at[0, everything], 10 * ph)
        pair_sum(0, a, n)
        go(mine.at[0, at_a], pass_in.at[0, at_a], k, to_up)
        pair_sum(0, b, n)
        go(mine.at[0, at_b], pass_in.at[1, at_b], k + 1, to_down)
        arrived(mate_in.at[1, everything], 10 * ph + 1)
        pair_sum(1, b, n)
        go(mine.at[1, at_b], done_in.at[0, at_b], k + 2, to_up)
        arrived(mate_in.at[2, everything], 10 * ph + 2)
        pair_sum(2, a, n)
        go(mine.at[2, at_a], done_in.at[1, at_a], k + 3, to_down)

    def pass_phase(ph):
        a, b, n, at_a, at_b, k = halves(ph)
        arrived(pass_in.at[0, at_a], k)
        pair_sum(1, a, n, 0)
        go(mine.at[1, at_a], done_in.at[0, at_a], k + 4, to_up)
        arrived(pass_in.at[1, at_b], k + 1)
        pair_sum(2, b, n, 1)
        go(mine.at[2, at_b], done_in.at[1, at_b], k + 5, to_down)

    def direct_phase(ph):
        lo, n = PHASES[ph]
        at = pl.ds(lo, n)
        for j, peer, slot in ((0, to_far, 2), (1, to_up, 0), (2, to_down, 1)):
            arrived(mate_in.at[j, at], 10 * ph + j)
            pair_sum(j, lo, n)
            go(mine.at[j, at], done_in.at[slot, at], 10 * ph + 4 + j, peer)

    def close_direct(ph):
        at = pl.ds(*PHASES[ph])
        arrived(mate_in.at[3, at], 10 * ph + 3)
        for j, slot in ((0, 2), (1, 0), (2, 1)):
            arrived(done_in.at[slot, at], 10 * ph + 4 + j)

    def close_phase(ph):
        a, b, n, at_a, at_b, k = halves(ph)
        arrived(mate_in.at[3, pl.ds(*PHASES[ph])], 10 * ph + 3)
        arrived(done_in.at[0, at_b], k + 2)
        arrived(done_in.at[1, at_a], k + 3)
        arrived(done_in.at[0, at_a], k + 4)
        arrived(done_in.at[1, at_b], k + 5)

    def whole(at):
        a = part[at, :, s] + mate_in[3, at]
        return a + done_in[0, at].astype(F32) + done_in[1, at].astype(F32)

    collect(0, CG, 0, 5, 7)
    to_the_mate(0)
    collect(CG, 2 * CG, CG, 5, 7)
    to_the_mate(1)
    collect(2 * CG, 3 * CG, -CG, 5, 7)
    to_the_mate(2)
    keep[1].wait()
    for i in range(4):
        garrived(xo.at[own, :, cols(mates[i])], 18 + i)
        garrived(xo.at[left_x, :, cols(mates[i])], 22 + i)
        garrived(xo.at[right_x, :, cols(mates[i])], 26 + i)
    open_phase(0)
    open_phase(1)
    run = far_segment(0, blank, True)
    open_phase(2)
    far_segment(1, run, True)
    pass_phase(0)
    pass_phase(1)
    near_all(True)
    pass_phase(2)
    collect(3 * CG, 4 * CG, -3 * CG, 6, 8)
    to_the_mate(3)
    direct_phase(3)
    close_phase(0)

    def edge(i, carry):
        at = pl.ds(i * chunk, chunk)
        side_out[at] = whole(at).astype(BF16)
        return carry

    lax.fori_loop(0, CG // chunk, edge, 0)
    go(side_out.at[pl.ds(0, CG)], side_in.at[0], 40, to_prev)
    close_phase(1)
    lax.fori_loop(CG // chunk, 2 * CG // chunk, edge, 0)
    go(side_out.at[pl.ds(CG, CG)], side_in.at[1], 41, to_next)
    close_phase(2)
    arrived(side_in.at[0], 40)
    arrived(side_in.at[1], 41)

    def own_adjoint(i, carry):
        at = i * chunk
        here = pl.ds(at, chunk)
        a = whole(pl.ds(2 * CG + at, chunk)) + side_in[0, here].astype(F32) + side_in[1, here].astype(F32)
        adj[here, 0] = a[:, 0]
        adj[here, 1] = -a[:, 1]
        return carry

    lax.fori_loop(0, CG // chunk, own_adjoint, 0)
    close_direct(3)

    def last(i, carry):
        here = pl.ds(i * chunk, chunk)
        at = pl.ds(3 * CG + i * chunk, chunk)
        f = whole(at) + done_in[2, at].astype(F32)
        fwd[here] = f
        prd = f[:, 0] * adj[here, 0] - f[:, 1] * adj[here, 1]
        sens[here] = jnp.sum(prd, axis=1) * (1.0 / (MEMBERS * COLS))
        return carry

    lax.fori_loop(0, CG // chunk, last, 0)

    sent = []
    for off in range(1, MEMBERS):
        d = pltpu.make_async_remote_copy(
            src_ref=sens, dst_ref=sgot.at[off - 1], send_sem=ssend.at[off - 1], recv_sem=srecv.at[off - 1],
            device_id={"sub": (s + off) % MEMBERS}, device_id_type=MESH,
        )
        d.start()
        sent.append(d)
    for d in sent:
        d.wait_recv()
    value = sens[...]
    for off in range(MEMBERS - 1):
        value = value + sgot[off]
    summed[...] = value
    KU = 4

    def clusters(i, acc):
        lhs = []
        for h in range(KU):
            k = i * KU + h
            at = pl.multiple_of(k * CS, CS)
            value, count = summed[pl.ds(k, 1), :], counts[pl.ds(k, 1), :]
            tops, rests = [], []
            for m in range(4):
                val = weights[pl.ds(m, 1), pl.ds(at, CS)] * value
                val = jnp.where(count > m, val, jnp.zeros_like(val))
                top = val.astype(BF16).astype(F32)
                hit = high_hot[k, :, m * CS : m * CS + CS]
                tops.append(hit * wide_of(top, GROUPS))
                rests.append(hit * wide_of(val - top, GROUPS))
            lhs.append(jnp.concatenate([jnp.concatenate(tops, axis=1), jnp.concatenate(rests, axis=1)], axis=0))
        made = [mm(lhs[h], low_hot[i * KU + h], NT) for h in range(KU)]
        for g in made:
            acc = acc + g
        return acc

    both = lax.fori_loop(0, CG // KU, clusters, jnp.zeros((2 * GROUPS, CS), F32))
    all_rows = both[:GROUPS] + both[GROUPS:]
    for k in range(GROUPS):
        row[k] = all_rows[k : k + 1]

    def ccopy(off):
        return pltpu.make_async_remote_copy(
            src_ref=row.at[(c + off) % GROUPS], dst_ref=ring.at[off - 1], send_sem=csend.at[off - 1],
            recv_sem=crecv.at[off - 1], device_id={"clus": (c + off) % GROUPS}, device_id_type=MESH,
        )

    def start(off, carry):
        ccopy(off).start()
        return carry

    def wait(off, carry):
        ccopy(off).wait()
        return carry

    lax.fori_loop(1, GROUPS, start, 0)
    for d in sent + started:
        d.wait_send()
    lax.fori_loop(1, GROUPS, wait, 0)
    final = row[c]
    for k in range(GROUPS - 1):
        final = final + ring[k]
    grad[...] = final


def hand_out(a, b, c, x, y, z):
    x[...] = a[...]
    y[...] = b[...]
    z[...] = c[...]


ANY = pl.BlockSpec(memory_space=pl.ANY)
VMEM = pl.BlockSpec(memory_space=pltpu.VMEM)


def split_form(x):
    n = x.shape[0]
    return x.reshape(n, COLS, 2, CS).transpose(0, 2, 1, 3)


def joined(x):
    n = x.shape[0]
    return x.transpose(0, 2, 1, 3).reshape(n, COLS, 2 * CS)


def shards(x, w, far_ids, ranks, far_left, far_right, near_ids, near, params, weights, counts):
    def sems(n):
        return pltpu.SemaphoreType.DMA((n,))

    half = (2, COLS, CS)
    fwd, adj, grad = pl.pallas_call(
        kernel,
        out_shape=(
            jax.ShapeDtypeStruct((CG,) + half, F32),
            jax.ShapeDtypeStruct((CG,) + half, F32),
            jax.ShapeDtypeStruct((1, CS), F32),
        ),
        in_specs=[ANY] * 5 + [VMEM] * 6,
        out_specs=(VMEM, VMEM, VMEM),
        scratch_shapes=[
            pltpu.VMEM((3 * CG, 2, MEMBERS * COLS, CS), BF16),
            pltpu.VMEM((CG, 2, MEMBERS * COLS, CS), BF16),
            pltpu.VMEM((FAR, 2, RANK, CS), BF16),
            pltpu.VMEM((FAR, 2, RANK, CS), BF16),
            pltpu.VMEM((NEAR, 2, CS, CS), BF16),
            pltpu.VMEM((8, FAR), jnp.int32),
            pltpu.VMEM((16, FAR), jnp.int32),
            pltpu.SMEM((16, FAR), jnp.int32),
            pltpu.VMEM((FAR + 1, MEMBERS * COLS, 2 * CS), F32),
            pltpu.VMEM((NEAR + 1, MEMBERS * COLS, 2 * CS), F32),
            pltpu.VMEM((WIDE, 2, MEMBERS, COLS, CS), F32),
            pltpu.VMEM((4, WIDE) + half, F32),
            pltpu.VMEM((3, WIDE) + half, BF16),
            pltpu.VMEM((2, WIDE) + half, BF16),
            pltpu.VMEM((3, WIDE) + half, BF16),
            pltpu.VMEM((2 * CG,) + half, BF16),
            pltpu.VMEM((2, CG) + half, BF16),
            pltpu.VMEM((CG, CS), F32),
            pltpu.VMEM((MEMBERS - 1, CG, CS), F32),
            pltpu.VMEM((CG, CS), F32),
            pltpu.VMEM((CG, GROUPS, 4 * CS), BF16),
            pltpu.VMEM((CG, CS, 4 * CS), BF16),
            pltpu.VMEM((GROUPS, 1, CS), F32),
            pltpu.VMEM((GROUPS - 1, 1, CS), F32),
            sems(6),
            sems(30),
            sems(30),
            sems(42),
            sems(42),
            sems(MEMBERS - 1),
            sems(MEMBERS - 1),
            sems(GROUPS - 1),
            sems(GROUPS - 1),
        ],
        compiler_params=pltpu.CompilerParams(collective_id=0, has_side_effects=True, vmem_limit_bytes=60 << 20),
        name="operator",
    )(
        split_form(x), split_form(w), far_left, far_right, near, far_ids, ranks.reshape(1, FAR), near_ids,
        params, weights, counts.reshape(CG, CS),
    )
    fwd, adj, grad = pl.pallas_call(
        hand_out,
        out_shape=tuple(jax.ShapeDtypeStruct(a.shape, a.dtype) for a in (fwd, adj, grad)),
        in_specs=[VMEM] * 3,
        out_specs=(VMEM,) * 3,
        name="hand_out",
    )(fwd, adj, grad)
    return joined(fwd), joined(adj), grad.reshape(CS)


def solution(mesh):
    rhs = P("clus", "sub", None)
    blocks = P(("clus", "sub"), None, None, None)
    both = ("clus", "sub")
    in_specs = (rhs, rhs, P(None, both), P(both), blocks, blocks, P(None, both), blocks)
    in_specs += (P(None, "clus"), P(None, "clus"), P("clus"))
    out_specs = (rhs, rhs, P(both))
    return jax.shard_map(shards, mesh=mesh, in_specs=in_specs, out_specs=out_specs, check_vma=False)
```
